32 devices in a mesh: dp: 2 (over core), seq: 4 (over y, x), head: 4 (over z).
Axes of the slice: x: 2, y: 2, z: 4, core: 2. Of those that a mesh axis runs over, the one named last changes fastest.
Arguments:
- query_rows: bfloat16 [2, 2048, 4096], P('dp', 'seq', 'head'), may hold values from -1.796875 to 1.796875
- key_rows: bfloat16 [2, 2048, 4096], P('dp', 'seq', 'head'), may hold values from -1.796875 to 1.796875
- value_rows: bfloat16 [2, 2048, 4096], P('dp', 'seq', 'head'), may hold values from -6 to 6
- norm_gain: float32 [4096], P('head'), may hold values from 0.1 to 1.9
- cotangent: bfloat16 [2, 2048, 4096], P('dp', 'seq', 'head'), may hold values from -10 to 10
- loss_mask: int32 [2, 2048], P('dp', 'seq'), may hold values 0 or 1
- importance: float32 [2, 2048], P('dp', 'seq'), may hold values from 0.5 to 2
- advantage: float32 [2], P('dp'), may hold values from -3 to 3
- lengths: int32 [2], P('dp'), may hold values from 512 to 2048, as said below
- decay_index: int32 [32], P('head'), may hold values from 0 to 11
Outputs:
- mixed: bfloat16 [2, 2048, 4096], P('dp', 'seq', 'head')
- query_grad: bfloat16 [2, 2048, 4096], P('dp', 'seq', 'head')
- key_grad: bfloat16 [2, 2048, 4096], P('dp', 'seq', 'head')
- value_grad: bfloat16 [2, 2048, 4096], P('dp', 'seq', 'head')
- gain_grad: float32 [4096], P('head')
The draws below stay inside these ranges and needn't reach their ends.
Inputs may be any that keep to these rules, and one draw needn't show every extreme that they name: `lengths`: at least one response has length 2048.
All inputs are finite; a program needn't handle non-finite values. No bound on the sum of `loss_mask` on one device may be relied on, other than what follows from the above.
Results may differ from the reference program's by a relative error of at most 0.0063.
Values sent between devices are 32-bit elements; how exact they have to be, the bound alone decides.
A program may use at most 128 MiB of HBM per device.

```python
import math
import jax
import jax.numpy as jnp
from jax import lax

HEAD_DIM = 128
TOK_DEV = 512
HEADS = 32
SEQ_LEN = 2048
BATCH = 2
N_SEQ = 4


def draw_cotangent(key, part):
    features = HEADS * HEAD_DIM
    order = jnp.arange(BATCH * SEQ_LEN, dtype=jnp.float32).reshape(BATCH, SEQ_LEN, 1)
    scale = 0.5 + order / (BATCH * SEQ_LEN - 1)
    base = jnp.clip(jax.random.normal(jax.random.fold_in(key, 13), (BATCH, SEQ_LEN, features), jnp.float32), -6.0, 6.0)
    values = base * scale
    return values.astype(jnp.bfloat16)


def draw_lengths(key, part):
    base = jax.random.randint(jax.random.fold_in(key, 21), (BATCH,), SEQ_LEN // 4, SEQ_LEN + 1, dtype=jnp.int32)
    chosen = jax.random.randint(jax.random.fold_in(key, 22), (), 0, BATCH, dtype=jnp.int32)
    rows = jnp.arange(BATCH, dtype=jnp.int32)
    return jnp.where(rows == chosen, jnp.int32(SEQ_LEN), base).astype(jnp.int32)


def place_ends(result, rng, smallest, largest):
    index_at = [jax.random.randint(jax.random.fold_in(rng, axis), (), 0, length) for axis, length in enumerate(result.shape)]
    main_axis = result.shape.index(max(result.shape))
    neighbour = index_at[:main_axis] + [(index_at[main_axis] + 1) % result.shape[main_axis]] + index_at[main_axis + 1:]
    return result.at[tuple(index_at)].set(smallest).at[tuple(neighbour)].set(largest)


def shard_levels(key, shape, split, least, top_value):
    def one(axis_at, blocks):
        steps = jax.random.uniform(jax.random.fold_in(jax.random.fold_in(key, 6), axis_at), (blocks,), jnp.float32, least / len(split), top_value / len(split))
        return jnp.repeat(jnp.exp(steps), shape[axis_at] // blocks).reshape((-1,) + (1,) * (len(shape) - axis_at - 1))

    factor_of = one(*split[0])
    for cut in split[1:]:
        factor_of = factor_of * one(*cut)
    return factor_of


def centred(stream_key, dims, scale, most, shards=(), held_as=jnp.bfloat16):
    loudness = shard_levels(stream_key, dims, shards, -0.22, 0.18) if shards else 1.0
    result = jax.random.normal(stream_key, dims, jnp.float32) * scale * loudness
    return jnp.minimum(jnp.maximum(result, -most), most).astype(held_as)


def setup_inputs(seed: int = 0) -> dict:
    streams_of = jax.random.split(jax.random.key(seed), 11)
    return {
        "query_rows": centred(streams_of[0], (BATCH, SEQ_LEN, HEADS * HEAD_DIM), 0.3, 1.796875, ((0, 2), (1, 4), (2, 4))),
        "key_rows": centred(streams_of[1], (BATCH, SEQ_LEN, HEADS * HEAD_DIM), 0.3, 1.796875, ((0, 2), (1, 4), (2, 4))),
        "value_rows": centred(streams_of[2], (BATCH, SEQ_LEN, HEADS * HEAD_DIM), 1.0, 6.0, ((0, 2), (1, 4), (2, 4))),
        "norm_gain": jnp.clip(1.0 + 0.18 * jax.random.normal(streams_of[3], (HEADS * HEAD_DIM,), jnp.float32), 0.1, 1.9),
        "cotangent": draw_cotangent(jax.random.fold_in(streams_of[10], 71), 0),
        "loss_mask": place_ends((jax.random.randint(streams_of[5], (BATCH, SEQ_LEN), 0, 4) < 3).astype(jnp.int32), jax.random.fold_in(streams_of[5], 1), 0, 1),
        "importance": jnp.clip(jnp.exp(math.log(2.0) - 1.3862944 * jax.random.uniform(streams_of[6], (BATCH, SEQ_LEN), jnp.float32) ** shard_levels(streams_of[6], (BATCH, SEQ_LEN), ((0, 2), (1, 4)), -0.2, 0.2)), 0.5, 2.0),
        "advantage": centred(streams_of[7], (BATCH,), 1.0, 3.0, ((0, 2),), jnp.float32),
        "lengths": draw_lengths(jax.random.fold_in(streams_of[10], 71), 0),
        "decay_index": place_ends(jax.random.randint(streams_of[9], (HEADS,), 0, 12), jax.random.fold_in(streams_of[9], 1), 0, 11).astype(jnp.int32),
    }


clip_high = 1.28
epsilon = 1e-06

def head_rates(decay_index):
    return 16.0 / (TOK_DEV * jnp.exp2(decay_index.astype(jnp.float32)))

def by_heads(array):
    return array.reshape(BATCH, N_SEQ, TOK_DEV, HEADS, HEAD_DIM).transpose(3, 0, 1, 2, 4)

def merge_heads(array):
    return array.transpose(1, 2, 3, 0, 4).reshape(BATCH, SEQ_LEN, HEADS * HEAD_DIM)

def decay_table(decay_rate):
    offsets = jnp.arange(TOK_DEV, dtype=jnp.float32)
    lagged = offsets[:, None] - offsets[None, :]
    within = jnp.where(lagged >= 0, jnp.exp2(-decay_rate * jnp.maximum(lagged, 0.0)), 0.0)
    return (offsets, within)

def carry_states(local_terms, factor, reverse):

    def advance(running, local_term):
        return (factor * running + local_term, running)
    zeros_state = jnp.zeros(local_terms.shape[1:], jnp.float32)
    _, passed = lax.scan(advance, zeros_state, local_terms, reverse=reverse)
    return passed

def forward_parts(queries, key_heads, value_heads, decay_rate):
    offsets, within = decay_table(decay_rate)
    scores = jnp.einsum('bntd,bnsd->bnts', queries.astype(jnp.float32), key_heads.astype(jnp.float32))
    score_half = (scores * within).astype(jnp.bfloat16)
    key_decayed = (key_heads.astype(jnp.float32) * jnp.exp2(-decay_rate * (TOK_DEV - 1 - offsets))[:, None]).astype(jnp.bfloat16)
    state_local = jnp.einsum('bntd,bnte->bnde', key_decayed.astype(jnp.float32), value_heads.astype(jnp.float32))
    passed = carry_states(state_local.transpose(1, 0, 2, 3), jnp.exp2(-decay_rate * TOK_DEV), False)
    state_half = passed.transpose(1, 0, 2, 3).astype(jnp.bfloat16)
    return (offsets, within, score_half, state_half)

def forward_head(queries, key_heads, value_heads, decay_rate):
    offsets, within, score_half, state_half = forward_parts(queries, key_heads, value_heads, decay_rate)
    local_out = jnp.einsum('bnts,bnse->bnte', score_half.astype(jnp.float32), value_heads.astype(jnp.float32))
    carried = jnp.einsum('bntd,bnde->bnte', queries.astype(jnp.float32), state_half.astype(jnp.float32))
    return local_out + carried * jnp.exp2(-decay_rate * (offsets + 1.0))[:, None]

def backward_head(queries, key_heads, value_heads, grad_heads, decay_rate):
    offsets, within, score_half, state_half = forward_parts(queries, key_heads, value_heads, decay_rate)
    f_query = queries.astype(jnp.float32)
    f_key = key_heads.astype(jnp.float32)
    f_value = value_heads.astype(jnp.float32)
    f_grad = grad_heads.astype(jnp.float32)
    dscore = (jnp.einsum('bnte,bnse->bnts', f_grad, f_value) * within).astype(jnp.bfloat16).astype(jnp.float32)
    query_decayed = (f_query * jnp.exp2(-decay_rate * offsets)[:, None]).astype(jnp.bfloat16)
    return_local = jnp.einsum('bntd,bnte->bnde', query_decayed.astype(jnp.float32), f_grad)
    passed = carry_states(return_local.transpose(1, 0, 2, 3), jnp.exp2(-decay_rate * TOK_DEV), True)
    return_half = passed.transpose(1, 0, 2, 3).astype(jnp.bfloat16).astype(jnp.float32)
    from_start = jnp.exp2(-decay_rate * (offsets + 1.0))[:, None]
    to_next = jnp.exp2(-decay_rate * (TOK_DEV - offsets))[:, None]
    query_grad = jnp.einsum('bnts,bnsd->bntd', dscore, f_key)
    query_grad = query_grad + jnp.einsum('bnte,bnde->bntd', f_grad, state_half.astype(jnp.float32)) * from_start
    key_grad = jnp.einsum('bnts,bntd->bnsd', dscore, f_query)
    key_grad = key_grad + jnp.einsum('bnte,bnde->bntd', f_value, return_half) * to_next
    value_grad = jnp.einsum('bnts,bnte->bnse', score_half.astype(jnp.float32), f_grad)
    value_grad = value_grad + jnp.einsum('bntd,bnde->bnte', f_key, return_half) * to_next
    return (query_grad, key_grad, value_grad)

def reference(query_rows, key_rows, value_rows, norm_gain, cotangent, loss_mask, importance, advantage, lengths, decay_index):
    decay_rates = head_rates(decay_index)
    query_heads = by_heads(query_rows)
    key_heads = by_heads(key_rows)
    value_heads = by_heads(value_rows)

    def forward_bundle(bundle):
        return forward_head(bundle[0], bundle[1], bundle[2], bundle[3])
    head_outs = lax.map(forward_bundle, (query_heads, key_heads, value_heads, decay_rates))
    outputs_flat = merge_heads(head_outs)
    features = HEADS * HEAD_DIM
    positions = jnp.arange(SEQ_LEN, dtype=jnp.int32)
    in_length = (positions[None, :] < lengths[:, None]).astype(jnp.float32)
    token_weight = loss_mask.astype(jnp.float32) * in_length * jnp.minimum(importance, clip_high)
    token_weight = token_weight * advantage[:, None] * (float(SEQ_LEN) / lengths.astype(jnp.float32))[:, None]
    grad_y = cotangent.astype(jnp.float32) * token_weight[..., None]
    grad_n = grad_y * norm_gain
    inverse = lax.rsqrt(lax.optimization_barrier(jnp.sum(outputs_flat * outputs_flat, -1)) / features + epsilon)
    normed = outputs_flat * inverse[..., None]
    mixed = (normed * norm_gain).astype(jnp.bfloat16)
    mean_term = lax.optimization_barrier(jnp.sum(grad_n * outputs_flat, -1)) * inverse / features
    grad_out = (inverse[..., None] * (grad_n - normed * mean_term[..., None])).astype(jnp.bfloat16)
    gain_grad = lax.optimization_barrier(jnp.sum(grad_y * normed, axis=(0, 1)))
    grad_heads = by_heads(grad_out)

    def backward_bundle(bundle):
        return backward_head(bundle[0], bundle[1], bundle[2], bundle[3], bundle[4])
    gradients = lax.map(backward_bundle, (query_heads, key_heads, value_heads, grad_heads, decay_rates))
    query_grad = merge_heads(gradients[0]).astype(jnp.bfloat16)
    key_grad = merge_heads(gradients[1]).astype(jnp.bfloat16)
    value_grad = merge_heads(gradients[2]).astype(jnp.bfloat16)
    return (mixed, query_grad, key_grad, value_grad, gain_grad)
```

```python
import functools

import jax
import jax.numpy as jnp
from jax import lax
from jax.experimental import pallas as pl
from jax.experimental.pallas import tpu as pltpu
from jax.sharding import PartitionSpec as P

clip_high = 1.28
epsilon = 1e-06
f32 = jnp.float32
bf16 = jnp.bfloat16
MESH = pl.DeviceIdType.MESH
TURN = 3


def dot(a, b, ca, cb):
    return lax.dot_general(a, b, (((ca,), (cb,)), ((), ())), preferred_element_type=f32)


def kernel(
    n_seq,
    n_head,
    n_dp,
    decay_hbm,
    adv_ref,
    len_ref,
    gain_hbm,
    mask_hbm,
    imp_hbm,
    q_hbm,
    k_hbm,
    v_hbm,
    c_hbm,
    o_mix,
    o_dq,
    o_dk,
    o_dv,
    gg_ref,
    decay_ref,
    gain_ref,
    mask_ref,
    imp_ref,
    q,
    k,
    v,
    c,
    out,
    go,
    pk,
    pv,
    probs0,
    probs1,
    dsc0,
    dsc1,
    wtab0,
    wtab1,
    up,
    down,
    squares,
    mixes,
    tot_f,
    rcv_f,
    tot_b,
    rcv_b,
    pref_f,
    pref_b,
    state,
    stat,
    gsum,
    grcv,
    in_sem,
    kv_sem,
    small_sem,
    fs_sem,
    fr_sem,
    bs_sem,
    br_sem,
    ss_sem,
    sr_sem,
    gs_sem,
    gr_sem,
    turn,
):
    slab, features = q.shape
    heads = decay_ref.shape[0]
    pairs = heads // 2
    dim = features // heads
    blk = min(256, slab)
    nblk = slab // blk
    stages = n_seq.bit_length() - 1
    square = stages == 2
    probs = (probs0, probs1)
    dsc = (dsc0, dsc1)
    wtab = (wtab0, wtab1)
    me = lax.axis_index("seq")
    mh = lax.axis_index("head")
    md = lax.axis_index("dp")
    back = n_seq - 1 - me
    forward = (tot_f, rcv_f, fs_sem, fr_sem, pref_f, me)
    backward = (tot_b, rcv_b, bs_sem, br_sem, pref_b, back)

    def partner(step):
        g = 1 << step
        bit = lax.rem(lax.div(me, g), 2)
        return me + g * (1 - 2 * bit)

    def kv_load(i, which):
        src, dst = ((k_hbm, k), (v_hbm, v))[which]
        span = pl.ds(pl.multiple_of(i * 2 * dim, 2 * dim), 2 * dim)
        return pltpu.make_async_copy(src.at[0, :, span], dst.at[:, span], kv_sem.at[which, i])

    loads = [
        pltpu.make_async_copy(src.at[0], dst, in_sem.at[i])
        for i, (src, dst) in enumerate(((q_hbm, q), (c_hbm, c)))
    ]
    small = [
        pltpu.make_async_copy(src, dst, small_sem.at[i])
        for i, (src, dst) in enumerate(
            (
                (decay_hbm, decay_ref),
                (gain_hbm, gain_ref),
                (mask_hbm, mask_ref),
                (imp_hbm, imp_ref),
            )
        )
    ]
    small[0].start()
    for i in range(pairs):
        kv_load(i, 0).start()
        kv_load(i, 1).start()
    for load in small[1:]:
        load.start()

    barrier = pltpu.get_barrier_semaphore()
    for s in range(stages):
        pl.semaphore_signal(barrier, inc=1, device_id={"seq": partner(s)}, device_id_type=MESH)
    for off in range(1, n_head):
        pl.semaphore_signal(
            barrier, inc=1, device_id={"head": lax.rem(mh + off, n_head)}, device_id_type=MESH
        )
    for off in range(1, n_dp):
        pl.semaphore_signal(
            barrier, inc=1, device_id={"dp": lax.rem(md + off, n_dp)}, device_id_type=MESH
        )

    def cols(h):
        return pl.ds(pl.multiple_of(h * dim, dim), dim)

    def rate(h, width):
        index = jnp.full((1, width), decay_ref[h], jnp.int32).astype(f32)
        return 16.0 / (slab * jnp.exp2(index))

    small[0].wait()
    base = min(128, slab)
    line = lax.broadcasted_iota(jnp.int32, (base, dim), 0).astype(f32)

    @pl.loop(0, heads)
    def _(h):
        r = rate(h, dim)
        rise = jnp.exp2(-r * line)
        fall = jnp.exp2(-r * (base - 1.0 - line))
        for b in range(slab // base):
            rows = pl.ds(b * base, base)
            up[h, rows, :] = rise * jnp.exp2(-r * float(b * base))
            down[h, rows, :] = fall * jnp.exp2(-r * float(slab - (b + 1) * base))

    def hop(d, s, h, bit, src=None):
        tot, rcv, send, recv, _, _ = d
        return pltpu.make_async_remote_copy(
            src_ref=tot.at[s, h] if src is None else src,
            dst_ref=rcv.at[s, h],
            send_sem=send.at[s, h],
            recv_sem=recv.at[s, h],
            device_id={"seq": partner(bit)},
            device_id_type=MESH,
        )

    def lower_only(s, place):
        return lax.div(place, 2 << s) == n_seq // (2 << s) - 1

    def is_upper(s, place):
        return lax.rem(lax.div(place, 1 << s), 2) == 1

    def sends(s, place):
        return jnp.logical_not(jnp.logical_and(is_upper(s, place), lower_only(s, place)))

    def takes(s, place):
        return jnp.logical_or(is_upper(s, place), jnp.logical_not(lower_only(s, place)))

    def begin(d, s, h):
        @pl.when(sends(s, d[5]))
        def _():
            hop(d, s, h, s).start()

    def accept(d, h, s):
        tot, rcv, _, _, pref, place = d

        @pl.when(takes(s, place))
        def _():
            hop(d, s, h, s).wait_recv()
            g = 1 << s
            r = rate(h, dim) * slab
            upper = jnp.full((1, dim), lax.rem(lax.div(place, g), 2), jnp.int32).astype(f32)
            inner = jnp.full((1, dim), lax.rem(place, g), jnp.int32).astype(f32)
            got = rcv[s, h]
            to_prefix = upper * jnp.exp2(-r * inner)
            if s == 0:
                pref[h] = to_prefix * got
            else:
                pref[h] = pref[h] + to_prefix * got
            if s + 1 < stages:
                whole = jnp.exp2(-r * g)
                from_got = upper * whole + (1.0 - upper)
                from_own = upper + (1.0 - upper) * whole
                tot[s + 1, h] = from_got * got + from_own * tot[s, h]

        if s + 1 < stages:
            begin(d, s + 1, h)

    def begin_pair(d, i):
        place = d[5]
        begin(d, 0, 2 * i)
        if square:

            @pl.when(place < 2)
            def _():
                hop(d, 0, 2 * i + 1, 1).start()
        else:
            begin(d, 0, 2 * i + 1)

    def begin_rest(d):
        if square:
            tot, place = d[0], d[5]

            @pl.when(place == 0)
            def _():
                @pl.loop(0, pairs)
                def _(i):
                    hop(d, 1, 2 * i + 1, 0, tot.at[0, 2 * i + 1]).start()

    def accept_pair(d, i):
        tot, rcv, _, _, pref, place = d
        accept(d, 2 * i, 0)
        h = 2 * i + 1
        if not square:
            accept(d, h, 0)
            return

        @pl.when(place == 3)
        def _():
            hop(d, 0, h, 1).wait_recv()
            hop(d, 1, h, 0, rcv.at[0, h]).start()
            pref[h] = jnp.exp2(-rate(h, dim) * slab) * rcv[0, h]

        @pl.when(place == 2)
        def _():
            hop(d, 0, h, 1).wait_recv()
            fade = jnp.exp2(-rate(h, dim) * slab)
            got = fade * rcv[0, h]
            tot[1, h] = tot[0, h] + fade * got
            pref[h] = got
            hop(d, 1, h, 0).start()

    def finish_pair(d, i):
        _, rcv, _, _, pref, place = d
        if stages > 1:
            accept(d, 2 * i, stages - 1)
        h = 2 * i + 1
        if square:

            @pl.when(place != 0)
            def _():
                hop(d, 1, h, 0).wait_recv()
                pref[h] = pref[h] + rcv[1, h]
        elif stages > 1:
            accept(d, h, stages - 1)

    def middle(d):
        for s in range(1, stages - 1):

            @pl.loop(0, heads)
            def _(h, s=s):
                accept(d, h, s)

    def settle(d):
        place = d[5]
        for s in range(stages):
            for odd in range(2):
                bit = stages - 1 - s if square and odd else s
                if not (square and odd):
                    cond = sends(s, place)
                elif s == 0:
                    cond = place < 2
                else:
                    cond = place != 1

                @pl.when(cond)
                def _(s=s, odd=odd, bit=bit):
                    @pl.loop(0, pairs)
                    def _(i):
                        hop(d, s, 2 * i + odd, bit).wait_send()

    def local(i):
        kv_load(i, 0).wait()
        kv_load(i, 1).wait()
        for odd in range(2):
            h = 2 * i + odd
            faded = (k[:, cols(h)].astype(f32) * down[h]).astype(bf16)
            tot_f[0, h] = dot(faded, v[:, cols(h)], 0, 0)

    local(0)
    for load in loads:
        load.start()
    pl.semaphore_wait(barrier, stages + n_head - 1 + n_dp - 1)
    first = md == 0

    @pl.when(first)
    def _():
        begin_pair(forward, 0)

    @pl.loop(1, pairs)
    def _(i):
        local(i)

        @pl.when(first)
        def _():
            begin_pair(forward, i)

    @pl.when(first)
    def _():
        begin_rest(forward)

    @pl.loop(0, heads)
    def _(h):
        pref_f[h] = jnp.zeros((dim, dim), f32)
        pref_b[h] = jnp.zeros((dim, dim), f32)

    loads[0].wait()

    t_at = lax.broadcasted_iota(jnp.int32, (blk, blk), 0)
    s_at = lax.broadcasted_iota(jnp.int32, (blk, blk), 1)
    shift = min(TURN, pairs - 1)

    @pl.loop(0, pairs)
    def _(i):
        for odd in range(2):
            h = 2 * i + odd
            r = rate(h, dim)
            place = lax.broadcasted_iota(jnp.int32, (1, dim), 1).astype(f32)
            front = up[h, pl.ds(0, blk), :]
            near = jnp.concatenate(
                [front * jnp.exp2(r * (place + float(b * dim))) for b in range(blk // dim)],
                axis=1,
            )
            wtab[odd][i, 0] = jnp.where(t_at >= s_at, near, 0.0)
            for d in range(1, nblk):
                away = jnp.exp2(-r * float(blk * d))
                wtab[odd][i, d] = near * jnp.concatenate([away] * (blk // dim), axis=1)
        for a in range(nblk):
            rows = pl.ds(a * blk, blk)
            for odd in range(2):
                h = 2 * i + odd
                for b in range(a + 1):
                    past = pl.ds(b * blk, blk)
                    score = dot(q[rows, cols(h)], k[past, cols(h)], 1, 1)
                    probs[odd][i, rows, past] = (score * wtab[odd][i, a - b]).astype(bf16)
        for a in range(nblk):
            rows = pl.ds(a * blk, blk)
            past = pl.ds(0, (a + 1) * blk)
            for odd in range(2):
                h = 2 * i + odd
                out[rows, cols(h)] = dot(probs[odd][i, rows, past], v[past, cols(h)], 1, 0)

        if n_dp > 1:

            @pl.when(jnp.logical_and(first, i == shift))
            def _():
                pl.semaphore_signal(turn, inc=1, device_id={"dp": 1 - md}, device_id_type=MESH)

            @pl.when(jnp.logical_and(jnp.logical_not(first), i == shift))
            def _():
                pl.semaphore_wait(turn, 1)

                @pl.loop(0, pairs)
                def _(p):
                    begin_pair(forward, p)

                begin_rest(forward)

        @pl.when(jnp.logical_and(first, i >= 1))
        def _():
            accept_pair(forward, i - 1)

    @pl.when(first)
    def _():
        accept_pair(forward, pairs - 1)

    @pl.when(jnp.logical_not(first))
    def _():
        @pl.loop(0, pairs)
        def _(i):
            accept_pair(forward, i)

    middle(forward)

    loads[1].wait()
    for load in small[1:]:
        load.wait()

    token = mask_ref[...].astype(f32)
    at = me * slab + lax.broadcasted_iota(jnp.int32, (1, slab), 1)
    length = jnp.full((1, slab), len_ref[0], jnp.int32)
    token = token * (at < length).astype(f32) * jnp.minimum(imp_ref[...], clip_high)
    token = token * adv_ref[0] * (float(slab * n_seq) / length.astype(f32))

    squares[...] = jnp.zeros((slab, dim), f32)
    mixes[...] = jnp.zeros((slab, dim), f32)

    @pl.loop(0, pairs)
    def _(i):
        finish_pair(forward, i)
        fulls = []
        for odd in range(2):
            h = 2 * i + odd
            half = pref_f[h].astype(bf16)
            state[h] = half
            grow = up[h] * jnp.exp2(-rate(h, dim))
            full = out[:, cols(h)] + dot(q[:, cols(h)], half, 1, 0) * grow
            out[:, cols(h)] = full
            fulls.append((full, c[:, cols(h)].astype(f32) * gain_ref[pl.ds(h, 1), :] * full))
        squares[...] += fulls[0][0] * fulls[0][0] + fulls[1][0] * fulls[1][0]
        mixes[...] += fulls[0][1] + fulls[1][1]

    stat[mh, 0:1, :] = jnp.sum(squares[...].T, axis=0, keepdims=True)
    stat[mh, 1:2, :] = jnp.sum(mixes[...].T, axis=0, keepdims=True) * token
    posts = [
        pltpu.make_async_remote_copy(
            src_ref=stat.at[mh],
            dst_ref=stat.at[mh],
            send_sem=ss_sem.at[off - 1],
            recv_sem=sr_sem.at[off - 1],
            device_id={"head": lax.rem(mh + off, n_head)},
            device_id_type=MESH,
        )
        for off in range(1, n_head)
    ]
    for post in posts:
        post.start()
    settle(forward)
    for post in posts:
        post.wait()
    sums = stat[0]
    for i in range(1, n_head):
        sums = sums + stat[i]
    count = features * n_head
    inverse = lax.rsqrt(sums[0:1] / count + epsilon)
    mean = inverse * (sums[1:2] / count)

    def column(row):
        return jnp.broadcast_to(row, (dim, slab)).T

    inv_col = column(inverse)
    give_col = column(inverse * token)
    take_col = column(inverse * inverse * mean)

    @pl.loop(0, pairs)
    def _(i):
        for odd in range(2):
            h = 2 * i + odd
            gain = gain_ref[pl.ds(h, 1), :]
            given = c[:, cols(h)].astype(f32) * give_col
            grad = (given * gain - take_col * out[:, cols(h)]).astype(bf16)
            go[:, cols(h)] = grad
            faded = (q[:, cols(h)].astype(f32) * up[h]).astype(bf16)
            tot_b[0, h] = dot(faded, grad, 0, 0)
        begin_pair(backward, i)

    begin_rest(backward)

    @pl.loop(0, heads)
    def _(h):
        gain = gain_ref[pl.ds(h, 1), :]
        full = out[:, cols(h)]
        given = c[:, cols(h)].astype(f32) * give_col
        o_mix[0, :, cols(h)] = (full * inv_col * gain).astype(bf16)
        gsum[0, pl.ds(h, 1), :] = jnp.sum(given * full, axis=0, keepdims=True)

    def gain_copy(s):
        target = {"dp": lax.rem(md + 1, n_dp)} if s == stages else {"seq": partner(s)}
        return pltpu.make_async_remote_copy(
            src_ref=gsum.at[s],
            dst_ref=grcv.at[s],
            send_sem=gs_sem.at[s],
            recv_sem=gr_sem.at[s],
            device_id=target,
            device_id_type=MESH,
        )

    rounds = stages + (1 if n_dp > 1 else 0)

    def gain_round(s):
        gain_copy(s).wait()
        gsum[s + 1] = gsum[s] + grcv[s]
        if s + 1 < rounds:
            gain_copy(s + 1).start()

    gain_copy(0).start()

    @pl.loop(0, pairs)
    def _(i):
        for a in range(nblk):
            rows = pl.ds(a * blk, blk)
            for odd in range(2):
                h = 2 * i + odd
                grad = go[rows, cols(h)]
                for b in range(a + 1):
                    past = pl.ds(b * blk, blk)
                    score = dot(grad, v[past, cols(h)], 1, 1)
                    dsc[odd][rows, past] = (score * wtab[odd][i, a - b]).astype(bf16)
        for a in range(nblk):
            rows = pl.ds(a * blk, blk)
            past = pl.ds(0, (a + 1) * blk)
            for odd in range(2):
                h = 2 * i + odd
                grow = up[h, rows, :] * jnp.exp2(-rate(h, dim))
                total = dot(dsc[odd][rows, past], k[past, cols(h)], 1, 0)
                total = total + dot(go[rows, cols(h)], state[h], 1, 1) * grow
                o_dq[0, rows, cols(h)] = total.astype(bf16)
        for b in range(nblk):
            past = pl.ds(b * blk, blk)
            rest = pl.ds(b * blk, slab - b * blk)
            for odd in range(2):
                h = 2 * i + odd
                pk[past, cols(h)] = dot(dsc[odd][rest, past], q[rest, cols(h)], 0, 0)
                pv[past, cols(h)] = dot(probs[odd][i, rest, past], go[rest, cols(h)], 0, 0)

        @pl.when(2 * i < pairs)
        def _():
            accept_pair(backward, 2 * i)

        @pl.when(2 * i + 1 < pairs)
        def _():
            accept_pair(backward, 2 * i + 1)

        @pl.when(i == pairs // 2)
        def _():
            gain_round(0)

    for s in range(1, rounds - 1):
        gain_round(s)
    middle(backward)

    @pl.loop(0, pairs)
    def _(i):
        finish_pair(backward, i)
        for odd in range(2):
            h = 2 * i + odd
            half = pref_b[h].astype(bf16)
            fade = down[h] * jnp.exp2(-rate(h, dim))
            dk = pk[:, cols(h)] + dot(v[:, cols(h)], half, 1, 1) * fade
            o_dk[0, :, cols(h)] = dk.astype(bf16)
            dv = pv[:, cols(h)] + dot(k[:, cols(h)], half, 1, 0) * fade
            o_dv[0, :, cols(h)] = dv.astype(bf16)

    if rounds > 1:
        gain_round(rounds - 1)
    gg_ref[...] = gsum[rounds]
    settle(backward)


def writer(n, *refs):
    sem = refs[-1]
    copies = [pltpu.make_async_copy(refs[i], refs[n + i], sem.at[i]) for i in range(n)]
    for copy in copies:
        copy.start()
    for copy in copies:
        copy.wait()


def on_device(
    n_seq,
    n_head,
    n_dp,
    query_rows,
    key_rows,
    value_rows,
    norm_gain,
    cotangent,
    loss_mask,
    importance,
    advantage,
    lengths,
    decay_index,
):
    batches, slab, features = query_rows.shape
    heads = decay_index.shape[0]
    dim = features // heads
    stages = n_seq.bit_length() - 1
    assert batches == 1 and heads % 2 == 0 and n_seq == 1 << stages and stages > 0 and n_dp <= 2
    vmem = pl.BlockSpec(memory_space=pltpu.VMEM)
    smem = pl.BlockSpec(memory_space=pltpu.SMEM)
    far = pl.BlockSpec(memory_space=pltpu.HBM)
    rows = jax.ShapeDtypeStruct(query_rows.shape, bf16)
    wide = pltpu.VMEM((slab, features), bf16)
    wide32 = pltpu.VMEM((slab, features), f32)
    blk = min(256, slab)
    states = pltpu.VMEM((stages, heads, dim, dim), f32)
    dma = pltpu.SemaphoreType.DMA

    def stay(array):
        return pltpu.with_memory_space_constraint(array, pltpu.HBM)

    results = pl.pallas_call(
        functools.partial(kernel, n_seq, n_head, n_dp),
        out_shape=(rows, rows, rows, rows, jax.ShapeDtypeStruct((heads, dim), f32)),
        in_specs=[far, smem, smem] + [far] * 7,
        out_specs=(vmem,) * 5,
        scratch_shapes=[
            pltpu.SMEM((heads,), jnp.int32),
            pltpu.VMEM((heads, dim), f32),
            pltpu.VMEM((1, slab), jnp.int32),
            pltpu.VMEM((1, slab), f32),
        ]
        + [wide] * 4
        + [wide32, wide, wide32, wide32]
        + [
            pltpu.VMEM((heads // 2, slab, slab), bf16),
            pltpu.VMEM((heads // 2, slab, slab), bf16),
            pltpu.VMEM((slab, slab), bf16),
            pltpu.VMEM((slab, slab), bf16),
            pltpu.VMEM((heads // 2, slab // blk, blk, blk), f32),
            pltpu.VMEM((heads // 2, slab // blk, blk, blk), f32),
            pltpu.VMEM((heads, slab, dim), f32),
            pltpu.VMEM((heads, slab, dim), f32),
            pltpu.VMEM((slab, dim), f32),
            pltpu.VMEM((slab, dim), f32),
            states,
            states,
            states,
            states,
            pltpu.VMEM((heads, dim, dim), f32),
            pltpu.VMEM((heads, dim, dim), f32),
            pltpu.VMEM((heads, dim, dim), bf16),
            pltpu.VMEM((n_head, 2, slab), f32),
            pltpu.VMEM((stages + 2, heads, dim), f32),
            pltpu.VMEM((stages + 1, heads, dim), f32),
            dma((2,)),
            dma((2, heads // 2)),
            dma((4,)),
            dma((stages, heads)),
            dma((stages, heads)),
            dma((stages, heads)),
            dma((stages, heads)),
            dma((max(n_head - 1, 1),)),
            dma((max(n_head - 1, 1),)),
            dma((stages + 1,)),
            dma((stages + 1,)),
            pltpu.SemaphoreType.REGULAR,
        ],
        compiler_params=pltpu.CompilerParams(
            collective_id=0, has_side_effects=True, vmem_limit_bytes=48 << 20
        ),
        name="lightning",
    )(
        stay(decay_index),
        advantage,
        lengths,
        stay(norm_gain.reshape(heads, dim)),
        stay(loss_mask),
        stay(importance),
        stay(query_rows),
        stay(key_rows),
        stay(value_rows),
        stay(cotangent),
    )
    shapes = tuple(jax.ShapeDtypeStruct(r.shape, r.dtype) for r in results)
    any_space = pl.BlockSpec(memory_space=pl.ANY)
    mixed, dq, dk, dv, gain_grad = pl.pallas_call(
        functools.partial(writer, len(shapes)),
        out_shape=shapes,
        in_specs=[vmem] * len(shapes),
        out_specs=(any_space,) * len(shapes),
        scratch_shapes=[dma((len(shapes),))],
        compiler_params=pltpu.CompilerParams(vmem_limit_bytes=8 << 20),
        name="writer",
    )(*results)
    return (mixed, dq, dk, dv, gain_grad.reshape(features))


def solution(mesh):
    wide = P("dp", "seq", "head")
    token = P("dp", "seq")
    in_specs = (wide, wide, wide, P("head"), wide, token, token, P("dp"), P("dp"), P("head"))
    out_specs = (wide, wide, wide, wide, P("head"))
    body = functools.partial(on_device, mesh.shape["seq"], mesh.shape["head"], mesh.shape["dp"])
    return jax.shard_map(
        body, mesh=mesh, in_specs=in_specs, out_specs=out_specs, check_vma=False
    )
```

```python
import functools

import jax
import jax.numpy as jnp
from jax import lax
from jax.experimental import pallas as pl
from jax.experimental.pallas import tpu as pltpu
from jax.sharding import PartitionSpec as P

clip_high = 1.28
epsilon = 1e-06
f32 = jnp.float32
bf16 = jnp.bfloat16
MESH = pl.DeviceIdType.MESH
TURN = 3


def dot(a, b, ca, cb):
    return lax.dot_general(a, b, (((ca,), (cb,)), ((), ())), preferred_element_type=f32)


def kernel(
    n_seq,
    n_head,
    n_dp,
    decay_hbm,
    adv_ref,
    len_ref,
    gain_hbm,
    mask_hbm,
    imp_hbm,
    q_hbm,
    k_hbm,
    v_hbm,
    c_hbm,
    o_mix,
    o_dq,
    o_dk,
    o_dv,
    gg_ref,
    decay_ref,
    gain_ref,
    mask_ref,
    imp_ref,
    q,
    k,
    v,
    c,
    out,
    go,
    pk,
    pv,
    probs0,
    probs1,
    dsc0,
    dsc1,
    wtab0,
    wtab1,
    up,
    down,
    squares,
    mixes,
    tot_f,
    rcv_f,
    tot_b,
    rcv_b,
    pref_f,
    pref_b,
    state,
    stat,
    gsum,
    gpair,
    in_sem,
    kv_sem,
    small_sem,
    fs_sem,
    fr_sem,
    bs_sem,
    br_sem,
    ss_sem,
    sr_sem,
    gs_sem,
    gr_sem,
    turn,
):
    slab, features = q.shape
    heads = decay_ref.shape[0]
    pairs = heads // 2
    dim = features // heads
    blk = min(256, slab)
    nblk = slab // blk
    stages = n_seq.bit_length() - 1
    square = stages == 2
    probs = (probs0, probs1)
    dsc = (dsc0, dsc1)
    wtab = (wtab0, wtab1)
    me = lax.axis_index("seq")
    mh = lax.axis_index("head")
    md = lax.axis_index("dp")
    back = n_seq - 1 - me
    forward = (tot_f, rcv_f, fs_sem, fr_sem, pref_f, me)
    backward = (tot_b, rcv_b, bs_sem, br_sem, pref_b, back)

    def partner(step):
        g = 1 << step
        bit = lax.rem(lax.div(me, g), 2)
        return me + g * (1 - 2 * bit)

    def kv_load(i, which):
        src, dst = ((k_hbm, k), (v_hbm, v))[which]
        span = pl.ds(pl.multiple_of(i * 2 * dim, 2 * dim), 2 * dim)
        return pltpu.make_async_copy(src.at[0, :, span], dst.at[:, span], kv_sem.at[which, i])

    loads = [
        pltpu.make_async_copy(src.at[0], dst, in_sem.at[i])
        for i, (src, dst) in enumerate(((q_hbm, q), (c_hbm, c)))
    ]
    small = [
        pltpu.make_async_copy(src, dst, small_sem.at[i])
        for i, (src, dst) in enumerate(
            (
                (decay_hbm, decay_ref),
                (gain_hbm, gain_ref),
                (mask_hbm, mask_ref),
                (imp_hbm, imp_ref),
            )
        )
    ]
    small[0].start()
    kv_load(0, 0).start()
    kv_load(0, 1).start()

    barrier = pltpu.get_barrier_semaphore()
    for off in range(1, n_seq):
        pl.semaphore_signal(
            barrier, inc=1, device_id={"seq": lax.rem(me + off, n_seq)}, device_id_type=MESH
        )
    for off in range(1, n_head):
        pl.semaphore_signal(
            barrier, inc=1, device_id={"head": lax.rem(mh + off, n_head)}, device_id_type=MESH
        )
    for off in range(1, n_dp):
        pl.semaphore_signal(
            barrier, inc=1, device_id={"dp": lax.rem(md + off, n_dp)}, device_id_type=MESH
        )

    for i in range(1, pairs):
        kv_load(i, 0).start()
        kv_load(i, 1).start()
    for load in small[1:]:
        load.start()

    def cols(h):
        return pl.ds(pl.multiple_of(h * dim, dim), dim)

    def rate(h, width):
        index = jnp.full((1, width), decay_ref[h], jnp.int32).astype(f32)
        return 16.0 / (slab * jnp.exp2(index))

    small[0].wait()
    base = min(128, slab)
    line = lax.broadcasted_iota(jnp.int32, (base, dim), 0).astype(f32)

    def falling(h):
        r = rate(h, dim)
        fall = jnp.exp2(-r * (base - 1.0 - line))
        for b in range(slab // base):
            rows = pl.ds(b * base, base)
            down[h, rows, :] = fall * jnp.exp2(-r * float(slab - (b + 1) * base))

    def rising(h):
        r = rate(h, dim)
        rise = jnp.exp2(-r * line)
        for b in range(slab // base):
            rows = pl.ds(b * base, base)
            up[h, rows, :] = rise * jnp.exp2(-r * float(b * base))

    def hop(d, s, h, bit, src=None):
        tot, rcv, send, recv, _, _ = d
        return pltpu.make_async_remote_copy(
            src_ref=tot.at[s, h] if src is None else src,
            dst_ref=rcv.at[s, h],
            send_sem=send.at[s, h],
            recv_sem=recv.at[s, h],
            device_id={"seq": partner(bit)},
            device_id_type=MESH,
        )

    def lower_only(s, place):
        return lax.div(place, 2 << s) == n_seq // (2 << s) - 1

    def is_upper(s, place):
        return lax.rem(lax.div(place, 1 << s), 2) == 1

    def sends(s, place):
        return jnp.logical_not(jnp.logical_and(is_upper(s, place), lower_only(s, place)))

    def takes(s, place):
        return jnp.logical_or(is_upper(s, place), jnp.logical_not(lower_only(s, place)))

    def begin(d, s, h):
        @pl.when(sends(s, d[5]))
        def _():
            hop(d, s, h, s).start()

    def accept(d, h, s):
        tot, rcv, _, _, pref, place = d

        @pl.when(takes(s, place))
        def _():
            hop(d, s, h, s).wait_recv()
            g = 1 << s
            r = rate(h, dim) * slab
            upper = jnp.full((1, dim), lax.rem(lax.div(place, g), 2), jnp.int32).astype(f32)
            inner = jnp.full((1, dim), lax.rem(place, g), jnp.int32).astype(f32)
            got = rcv[s, h]
            to_prefix = upper * jnp.exp2(-r * inner)
            if s == 0:
                pref[h] = to_prefix * got
            else:
                pref[h] = pref[h] + to_prefix * got
            if s + 1 < stages:
                whole = jnp.exp2(-r * g)
                from_got = upper * whole + (1.0 - upper)
                from_own = upper + (1.0 - upper) * whole
                tot[s + 1, h] = from_got * got + from_own * tot[s, h]

        if s + 1 < stages:
            begin(d, s + 1, h)

    def begin_even(d, i):
        begin(d, 0, 2 * i)

    def begin_odd(d, i):
        place = d[5]
        if square:

            @pl.when(place < 2)
            def _():
                hop(d, 0, 2 * i + 1, 1).start()
        else:
            begin(d, 0, 2 * i + 1)

    def begin_pair(d, i):
        begin_even(d, i)
        begin_odd(d, i)

    def begin_rest(d):
        if square:
            tot, place = d[0], d[5]

            @pl.when(place == 0)
            def _():
                @pl.loop(0, pairs)
                def _(i):
                    hop(d, 1, 2 * i + 1, 0, tot.at[0, 2 * i + 1]).start()

    def accept_pair(d, i):
        tot, rcv, _, _, pref, place = d
        accept(d, 2 * i, 0)
        h = 2 * i + 1
        if not square:
            accept(d, h, 0)
            return

        @pl.when(place == 3)
        def _():
            hop(d, 0, h, 1).wait_recv()
            hop(d, 1, h, 0, rcv.at[0, h]).start()
            pref[h] = jnp.exp2(-rate(h, dim) * slab) * rcv[0, h]

        @pl.when(place == 2)
        def _():
            hop(d, 0, h, 1).wait_recv()
            fade = jnp.exp2(-rate(h, dim) * slab)
            got = fade * rcv[0, h]
            tot[1, h] = tot[0, h] + fade * got
            pref[h] = got
            hop(d, 1, h, 0).start()

    def finish_even(d, i):
        if stages > 1:
            accept(d, 2 * i, stages - 1)

    def finish_odd(d, i):
        _, rcv, _, _, pref, place = d
        h = 2 * i + 1
        if square:

            @pl.when(place != 0)
            def _():
                hop(d, 1, h, 0).wait_recv()
                pref[h] = pref[h] + rcv[1, h]
        elif stages > 1:
            accept(d, h, stages - 1)

    def middle(d):
        for s in range(1, stages - 1):

            @pl.loop(0, heads)
            def _(h, s=s):
                accept(d, h, s)

    def settle(d):
        place = d[5]
        for s in range(stages):
            for odd in range(2):
                bit = stages - 1 - s if square and odd else s
                if not (square and odd):
                    cond = sends(s, place)
                elif s == 0:
                    cond = place < 2
                else:
                    cond = place != 1

                @pl.when(cond)
                def _(s=s, odd=odd, bit=bit):
                    @pl.loop(0, pairs)
                    def _(i):
                        hop(d, s, 2 * i + odd, bit).wait_send()

    def local(i):
        falling(2 * i)
        falling(2 * i + 1)
        kv_load(i, 0).wait()
        kv_load(i, 1).wait()
        for odd in range(2):
            h = 2 * i + odd
            faded = (k[:, cols(h)].astype(f32) * down[h]).astype(bf16)
            tot_f[0, h] = dot(faded, v[:, cols(h)], 0, 0)

    local(0)
    for load in loads:
        load.start()
    pl.semaphore_wait(barrier, n_seq - 1 + n_head - 1 + n_dp - 1)
    first = md == 0

    @pl.when(first)
    def _():
        begin_pair(forward, 0)

    @pl.loop(1, pairs)
    def _(i):
        local(i)

        @pl.when(first)
        def _():
            begin_pair(forward, i)

    @pl.when(first)
    def _():
        begin_rest(forward)

    @pl.loop(0, heads)
    def _(h):
        rising(h)
        pref_f[h] = jnp.zeros((dim, dim), f32)
        pref_b[h] = jnp.zeros((dim, dim), f32)

    loads[0].wait()

    t_at = lax.broadcasted_iota(jnp.int32, (blk, blk), 0)
    s_at = lax.broadcasted_iota(jnp.int32, (blk, blk), 1)
    shift = min(TURN, pairs - 1)

    @pl.loop(0, pairs)
    def _(i):
        for odd in range(2):
            h = 2 * i + odd
            r = rate(h, dim)
            place = lax.broadcasted_iota(jnp.int32, (1, dim), 1).astype(f32)
            front = up[h, pl.ds(0, blk), :]
            near = jnp.concatenate(
                [front * jnp.exp2(r * (place + float(b * dim))) for b in range(blk // dim)],
                axis=1,
            )
            wtab[odd][i, 0] = jnp.where(t_at >= s_at, near, 0.0)
            for d in range(1, nblk):
                away = jnp.exp2(-r * float(blk * d))
                wtab[odd][i, d] = near * jnp.concatenate([away] * (blk // dim), axis=1)
        for a in range(nblk):
            rows = pl.ds(a * blk, blk)
            for odd in range(2):
                h = 2 * i + odd
                for b in range(a + 1):
                    past = pl.ds(b * blk, blk)
                    score = dot(q[rows, cols(h)], k[past, cols(h)], 1, 1)
                    probs[odd][i, rows, past] = (score * wtab[odd][i, a - b]).astype(bf16)
        for a in range(nblk):
            rows = pl.ds(a * blk, blk)
            past = pl.ds(0, (a + 1) * blk)
            for odd in range(2):
                h = 2 * i + odd
                out[rows, cols(h)] = dot(probs[odd][i, rows, past], v[past, cols(h)], 1, 0)

        for ahead in (1, 0):

            @pl.when(jnp.logical_and(first, (2 * i - ahead >= 0) & (2 * i - ahead < pairs)))
            def _(ahead=ahead):
                accept_pair(forward, 2 * i - ahead)

        if n_dp > 1:

            @pl.when(jnp.logical_and(first, i == shift))
            def _():
                pl.semaphore_signal(turn, inc=1, device_id={"dp": 1 - md}, device_id_type=MESH)

            @pl.when(jnp.logical_and(jnp.logical_not(first), i == shift))
            def _():
                pl.semaphore_wait(turn, 1)

                @pl.loop(0, pairs)
                def _(p):
                    begin_pair(forward, p)

                begin_rest(forward)

    @pl.when(jnp.logical_not(first))
    def _():
        @pl.loop(0, pairs)
        def _(i):
            accept_pair(forward, i)

    middle(forward)

    loads[1].wait()
    for load in small[1:]:
        load.wait()

    token = mask_ref[...].astype(f32)
    at = me * slab + lax.broadcasted_iota(jnp.int32, (1, slab), 1)
    length = jnp.full((1, slab), len_ref[0], jnp.int32)
    token = token * (at < length).astype(f32) * jnp.minimum(imp_ref[...], clip_high)
    token = token * adv_ref[0] * (float(slab * n_seq) / length.astype(f32))

    squares[...] = jnp.zeros((slab, dim), f32)
    mixes[...] = jnp.zeros((slab, dim), f32)

    def widen(h):
        half = pref_f[h].astype(bf16)
        state[h] = half
        grow = up[h] * jnp.exp2(-rate(h, dim))
        full = out[:, cols(h)] + dot(q[:, cols(h)], half, 1, 0) * grow
        out[:, cols(h)] = full
        return full, c[:, cols(h)].astype(f32) * gain_ref[pl.ds(h, 1), :] * full

    @pl.loop(0, pairs - 1)
    def _(i):
        finish_even(forward, i)
        finish_odd(forward, i)
        full, mix = widen(2 * i)
        other, blend = widen(2 * i + 1)
        squares[...] += full * full + other * other
        mixes[...] += mix + blend

    finish_even(forward, pairs - 1)
    full, mix = widen(heads - 2)
    squares[...] += full * full
    mixes[...] += mix
    finish_odd(forward, pairs - 1)
    full, mix = widen(heads - 1)
    squares[...] += full * full
    mixes[...] += mix

    stat[mh, 0:1, :] = jnp.sum(squares[...].T, axis=0, keepdims=True)
    stat[mh, 1:2, :] = jnp.sum(mixes[...].T, axis=0, keepdims=True) * token
    posts = [
        pltpu.make_async_remote_copy(
            src_ref=stat.at[mh],
            dst_ref=stat.at[mh],
            send_sem=ss_sem.at[off - 1],
            recv_sem=sr_sem.at[off - 1],
            device_id={"head": lax.rem(mh + off, n_head)},
            device_id_type=MESH,
        )
        for off in range(1, n_head)
    ]
    for post in posts:
        post.start()
    for post in posts:
        post.wait_recv()
    sums = stat[0]
    for i in range(1, n_head):
        sums = sums + stat[i]
    count = features * n_head
    inverse = lax.rsqrt(sums[0:1] / count + epsilon)
    mean = inverse * (sums[1:2] / count)

    def column(row):
        return jnp.broadcast_to(row, (dim, slab)).T

    inv_col = column(inverse)
    give_col = column(inverse * token)
    take_col = column(inverse * inverse * mean)

    def give(h):
        given = c[:, cols(h)].astype(f32) * give_col
        grad = (given * gain_ref[pl.ds(h, 1), :] - take_col * out[:, cols(h)]).astype(bf16)
        go[:, cols(h)] = grad
        faded = (q[:, cols(h)].astype(f32) * up[h]).astype(bf16)
        tot_b[0, h] = dot(faded, grad, 0, 0)

    give(0)
    begin_even(backward, 0)
    give(1)
    begin_odd(backward, 0)

    @pl.loop(1, pairs)
    def _(i):
        give(2 * i)
        give(2 * i + 1)
        begin_even(backward, i)
        begin_odd(backward, i)

    begin_rest(backward)

    @pl.loop(0, heads)
    def _(h):
        gain = gain_ref[pl.ds(h, 1), :]
        full = out[:, cols(h)]
        given = c[:, cols(h)].astype(f32) * give_col
        o_mix[0, :, cols(h)] = (full * inv_col * gain).astype(bf16)
        gsum[me, pl.ds(h, 1), :] = jnp.sum(given * full, axis=0, keepdims=True)

    shares = [
        pltpu.make_async_remote_copy(
            src_ref=gsum.at[me],
            dst_ref=gsum.at[me],
            send_sem=gs_sem.at[off],
            recv_sem=gr_sem.at[off],
            device_id={"seq": lax.rem(me + off, n_seq)},
            device_id_type=MESH,
        )
        for off in range(1, n_seq)
    ]
    swap = pltpu.make_async_remote_copy(
        src_ref=gpair.at[0],
        dst_ref=gpair.at[1],
        send_sem=gs_sem.at[0],
        recv_sem=gr_sem.at[0],
        device_id={"dp": lax.rem(md + 1, n_dp)},
        device_id_type=MESH,
    )
    for share in shares:
        share.start()
    accept_pair(backward, 0)

    @pl.loop(0, pairs)
    def _(i):
        for a in range(nblk):
            rows = pl.ds(a * blk, blk)
            for odd in range(2):
                h = 2 * i + odd
                grad = go[rows, cols(h)]
                for b in range(a + 1):
                    past = pl.ds(b * blk, blk)
                    score = dot(grad, v[past, cols(h)], 1, 1)
                    dsc[odd][rows, past] = (score * wtab[odd][i, a - b]).astype(bf16)
        for a in range(nblk):
            rows = pl.ds(a * blk, blk)
            past = pl.ds(0, (a + 1) * blk)
            for odd in range(2):
                h = 2 * i + odd
                grow = up[h, rows, :] * jnp.exp2(-rate(h, dim))
                total = dot(dsc[odd][rows, past], k[past, cols(h)], 1, 0)
                total = total + dot(go[rows, cols(h)], state[h], 1, 1) * grow
                o_dq[0, rows, cols(h)] = total.astype(bf16)
        for b in range(nblk):
            past = pl.ds(b * blk, blk)
            rest = pl.ds(b * blk, slab - b * blk)
            for odd in range(2):
                h = 2 * i + odd
                pk[past, cols(h)] = dot(dsc[odd][rest, past], q[rest, cols(h)], 0, 0)
                pv[past, cols(h)] = dot(probs[odd][i, rest, past], go[rest, cols(h)], 0, 0)

        for ahead in (1, 2):

            @pl.when(2 * i + ahead < pairs)
            def _(ahead=ahead):
                accept_pair(backward, 2 * i + ahead)

    for share in shares:
        share.wait_recv()
    total = gsum[0]
    for s in range(1, n_seq):
        total = total + gsum[s]
    gpair[0] = total
    if n_dp > 1:
        swap.start()
    middle(backward)

    def close(h):
        half = pref_b[h].astype(bf16)
        fade = down[h] * jnp.exp2(-rate(h, dim))
        dk = pk[:, cols(h)] + dot(v[:, cols(h)], half, 1, 1) * fade
        o_dk[0, :, cols(h)] = dk.astype(bf16)
        dv = pv[:, cols(h)] + dot(k[:, cols(h)], half, 1, 0) * fade
        o_dv[0, :, cols(h)] = dv.astype(bf16)

    @pl.loop(0, pairs - 1)
    def _(i):
        finish_even(backward, i)
        finish_odd(backward, i)
        close(2 * i)
        close(2 * i + 1)

    finish_even(backward, pairs - 1)
    close(heads - 2)
    finish_odd(backward, pairs - 1)
    close(heads - 1)
    if n_dp > 1:
        swap.wait()
        gg_ref[...] = gpair[0] + gpair[1]
    else:
        gg_ref[...] = gpair[0]
    for post in posts + shares:
        post.wait_send()
    settle(forward)
    settle(backward)


def writer(n, *refs):
    sem = refs[-1]
    copies = [pltpu.make_async_copy(refs[i], refs[n + i], sem.at[i]) for i in range(n)]
    for copy in copies:
        copy.start()
    for copy in copies:
        copy.wait()


def on_device(
    n_seq,
    n_head,
    n_dp,
    query_rows,
    key_rows,
    value_rows,
    norm_gain,
    cotangent,
    loss_mask,
    importance,
    advantage,
    lengths,
    decay_index,
):
    batches, slab, features = query_rows.shape
    heads = decay_index.shape[0]
    dim = features // heads
    stages = n_seq.bit_length() - 1
    assert batches == 1 and heads % 2 == 0 and n_seq == 1 << stages and stages > 0 and n_dp <= 2
    vmem = pl.BlockSpec(memory_space=pltpu.VMEM)
    smem = pl.BlockSpec(memory_space=pltpu.SMEM)
    far = pl.BlockSpec(memory_space=pltpu.HBM)
    rows = jax.ShapeDtypeStruct(query_rows.shape, bf16)
    wide = pltpu.VMEM((slab, features), bf16)
    wide32 = pltpu.VMEM((slab, features), f32)
    blk = min(256, slab)
    states = pltpu.VMEM((stages, heads, dim, dim), f32)
    dma = pltpu.SemaphoreType.DMA

    def stay(array):
        return pltpu.with_memory_space_constraint(array, pltpu.HBM)

    results = pl.pallas_call(
        functools.partial(kernel, n_seq, n_head, n_dp),
        out_shape=(rows, rows, rows, rows, jax.ShapeDtypeStruct((heads, dim), f32)),
        in_specs=[far, smem, smem] + [far] * 7,
        out_specs=(vmem,) * 5,
        scratch_shapes=[
            pltpu.SMEM((heads,), jnp.int32),
            pltpu.VMEM((heads, dim), f32),
            pltpu.VMEM((1, slab), jnp.int32),
            pltpu.VMEM((1, slab), f32),
        ]
        + [wide] * 4
        + [wide32, wide, wide32, wide32]
        + [
            pltpu.VMEM((heads // 2, slab, slab), bf16),
            pltpu.VMEM((heads // 2, slab, slab), bf16),
            pltpu.VMEM((slab, slab), bf16),
            pltpu.VMEM((slab, slab), bf16),
            pltpu.VMEM((heads // 2, slab // blk, blk, blk), f32),
            pltpu.VMEM((heads // 2, slab // blk, blk, blk), f32),
            pltpu.VMEM((heads, slab, dim), f32),
            pltpu.VMEM((heads, slab, dim), f32),
            pltpu.VMEM((slab, dim), f32),
            pltpu.VMEM((slab, dim), f32),
            states,
            states,
            states,
            states,
            pltpu.VMEM((heads, dim, dim), f32),
            pltpu.VMEM((heads, dim, dim), f32),
            pltpu.VMEM((heads, dim, dim), bf16),
            pltpu.VMEM((n_head, 2, slab), f32),
            pltpu.VMEM((n_seq, heads, dim), f32),
            pltpu.VMEM((2, heads, dim), f32),
            dma((2,)),
            dma((2, heads // 2)),
            dma((4,)),
            dma((stages, heads)),
            dma((stages, heads)),
            dma((stages, heads)),
            dma((stages, heads)),
            dma((max(n_head - 1, 1),)),
            dma((max(n_head - 1, 1),)),
            dma((n_seq,)),
            dma((n_seq,)),
            pltpu.SemaphoreType.REGULAR,
        ],
        compiler_params=pltpu.CompilerParams(
            collective_id=0, has_side_effects=True, vmem_limit_bytes=48 << 20
        ),
        name="lightning",
    )(
        stay(decay_index),
        advantage,
        lengths,
        stay(norm_gain.reshape(heads, dim)),
        stay(loss_mask),
        stay(importance),
        stay(query_rows),
        stay(key_rows),
        stay(value_rows),
        stay(cotangent),
    )
    shapes = tuple(jax.ShapeDtypeStruct(r.shape, r.dtype) for r in results)
    any_space = pl.BlockSpec(memory_space=pl.ANY)
    mixed, dq, dk, dv, gain_grad = pl.pallas_call(
        functools.partial(writer, len(shapes)),
        out_shape=shapes,
        in_specs=[vmem] * len(shapes),
        out_specs=(any_space,) * len(shapes),
        scratch_shapes=[dma((len(shapes),))],
        compiler_params=pltpu.CompilerParams(vmem_limit_bytes=8 << 20),
        name="writer",
    )(*results)
    return (mixed, dq, dk, dv, gain_grad.reshape(features))


def solution(mesh):
    wide = P("dp", "seq", "head")
    token = P("dp", "seq")
    in_specs = (wide, wide, wide, P("head"), wide, token, token, P("dp"), P("dp"), P("head"))
    out_specs = (wide, wide, wide, wide, P("head"))
    body = functools.partial(on_device, mesh.shape["seq"], mesh.shape["head"], mesh.shape["dp"])
    return jax.shard_map(
        body, mesh=mesh, in_specs=in_specs, out_specs=out_specs, check_vma=False
    )
```

```python
import functools

import jax
import jax.numpy as jnp
from jax import lax
from jax.experimental import pallas as pl
from jax.experimental.pallas import tpu as pltpu
from jax.sharding import PartitionSpec as P

clip_high = 1.28
epsilon = 1e-06
f32 = jnp.float32
bf16 = jnp.bfloat16
MESH = pl.DeviceIdType.MESH
TURN = 3


def dot(a, b, ca, cb):
    return lax.dot_general(a, b, (((ca,), (cb,)), ((), ())), preferred_element_type=f32)


def kernel(
    n_seq,
    n_head,
    n_dp,
    decay_hbm,
    adv_ref,
    len_ref,
    gain_hbm,
    mask_hbm,
    imp_hbm,
    q_hbm,
    k_hbm,
    v_hbm,
    c_hbm,
    o_mix,
    o_dq,
    o_dk,
    o_dv,
    gg_ref,
    decay_ref,
    gain_ref,
    mask_ref,
    imp_ref,
    q,
    k,
    v,
    c,
    out,
    go,
    pk,
    pv,
    probs0,
    probs1,
    dsc0,
    dsc1,
    wtab0,
    wtab1,
    up,
    down,
    squares,
    mixes,
    tot_f,
    rcv_f,
    tot_b,
    rcv_b,
    pref_f,
    pref_b,
    state,
    stat,
    gsum,
    gpair,
    in_sem,
    kv_sem,
    small_sem,
    fs_sem,
    fr_sem,
    bs_sem,
    br_sem,
    ss_sem,
    sr_sem,
    gs_sem,
    gr_sem,
    turn,
    ready,
):
    slab, features = q.shape
    heads = decay_ref.shape[0]
    pairs = heads // 2
    dim = features // heads
    blk = min(256, slab)
    nblk = slab // blk
    stages = n_seq.bit_length() - 1
    square = stages == 2
    probs = (probs0, probs1)
    dsc = (dsc0, dsc1)
    wtab = (wtab0, wtab1)
    me = lax.axis_index("seq")
    mh = lax.axis_index("head")
    md = lax.axis_index("dp")
    back = n_seq - 1 - me
    forward = (tot_f, rcv_f, fs_sem, fr_sem, pref_f, me)
    backward = (tot_b, rcv_b, bs_sem, br_sem, pref_b, back)

    def partner(step):
        g = 1 << step
        bit = lax.rem(lax.div(me, g), 2)
        return me + g * (1 - 2 * bit)

    def kv_load(i, which):
        src, dst = ((k_hbm, k), (v_hbm, v))[which]
        span = pl.ds(pl.multiple_of(i * 2 * dim, 2 * dim), 2 * dim)
        return pltpu.make_async_copy(src.at[0, :, span], dst.at[:, span], kv_sem.at[which, i])

    loads = [
        pltpu.make_async_copy(src.at[0], dst, in_sem.at[i])
        for i, (src, dst) in enumerate(((q_hbm, q), (c_hbm, c)))
    ]
    small = [
        pltpu.make_async_copy(src, dst, small_sem.at[i])
        for i, (src, dst) in enumerate(
            (
                (decay_hbm, decay_ref),
                (gain_hbm, gain_ref),
                (mask_hbm, mask_ref),
                (imp_hbm, imp_ref),
            )
        )
    ]
    small[0].start()
    kv_load(0, 0).start()
    kv_load(0, 1).start()

    barrier = pltpu.get_barrier_semaphore()
    if square:
        for s in range(stages):
            pl.semaphore_signal(barrier, inc=1, device_id={"seq": partner(s)}, device_id_type=MESH)
    else:
        for off in range(1, n_seq):
            pl.semaphore_signal(
                barrier, inc=1, device_id={"seq": lax.rem(me + off, n_seq)}, device_id_type=MESH
            )
    near_heads = (mh > 0).astype(jnp.int32) + (mh < n_head - 1).astype(jnp.int32)

    def greet(sem):
        @pl.when(mh > 0)
        def _():
            pl.semaphore_signal(sem, inc=1, device_id={"head": mh - 1}, device_id_type=MESH)

        @pl.when(mh < n_head - 1)
        def _():
            pl.semaphore_signal(sem, inc=1, device_id={"head": mh + 1}, device_id_type=MESH)

    greet(barrier)
    for off in range(1, n_dp):
        pl.semaphore_signal(
            barrier, inc=1, device_id={"dp": lax.rem(md + off, n_dp)}, device_id_type=MESH
        )

    for i in range(1, pairs):
        kv_load(i, 0).start()
        kv_load(i, 1).start()
    for load in small[1:]:
        load.start()

    def cols(h):
        return pl.ds(pl.multiple_of(h * dim, dim), dim)

    def rate(h, width):
        index = jnp.full((1, width), decay_ref[h], jnp.int32).astype(f32)
        return 16.0 / (slab * jnp.exp2(index))

    small[0].wait()
    base = min(128, slab)
    line = lax.broadcasted_iota(jnp.int32, (base, dim), 0).astype(f32)

    def falling(h):
        r = rate(h, dim)
        fall = jnp.exp2(-r * (base - 1.0 - line))
        for b in range(slab // base):
            rows = pl.ds(b * base, base)
            down[h, rows, :] = fall * jnp.exp2(-r * float(slab - (b + 1) * base))

    def rising(h):
        r = rate(h, dim)
        rise = jnp.exp2(-r * line)
        for b in range(slab // base):
            rows = pl.ds(b * base, base)
            up[h, rows, :] = rise * jnp.exp2(-r * float(b * base))

    def hop(d, s, h, bit, src=None):
        tot, rcv, send, recv, _, _ = d
        return pltpu.make_async_remote_copy(
            src_ref=tot.at[s, h] if src is None else src,
            dst_ref=rcv.at[s, h],
            send_sem=send.at[s, h],
            recv_sem=recv.at[s, h],
            device_id={"seq": partner(bit)},
            device_id_type=MESH,
        )

    def lower_only(s, place):
        return lax.div(place, 2 << s) == n_seq // (2 << s) - 1

    def is_upper(s, place):
        return lax.rem(lax.div(place, 1 << s), 2) == 1

    def sends(s, place):
        return jnp.logical_not(jnp.logical_and(is_upper(s, place), lower_only(s, place)))

    def takes(s, place):
        return jnp.logical_or(is_upper(s, place), jnp.logical_not(lower_only(s, place)))

    def begin(d, s, h):
        @pl.when(sends(s, d[5]))
        def _():
            hop(d, s, h, s).start()

    def accept(d, h, s):
        tot, rcv, _, _, pref, place = d

        @pl.when(takes(s, place))
        def _():
            hop(d, s, h, s).wait_recv()
            g = 1 << s
            r = rate(h, dim) * slab
            upper = jnp.full((1, dim), lax.rem(lax.div(place, g), 2), jnp.int32).astype(f32)
            inner = jnp.full((1, dim), lax.rem(place, g), jnp.int32).astype(f32)
            got = rcv[s, h]
            to_prefix = upper * jnp.exp2(-r * inner)
            if s == 0:
                pref[h] = to_prefix * got
            else:
                pref[h] = pref[h] + to_prefix * got
            if s + 1 < stages:
                whole = jnp.exp2(-r * g)
                from_got = upper * whole + (1.0 - upper)
                from_own = upper + (1.0 - upper) * whole
                tot[s + 1, h] = from_got * got + from_own * tot[s, h]

        if s + 1 < stages:
            begin(d, s + 1, h)

    def begin_even(d, i):
        begin(d, 0, 2 * i)

    def begin_odd(d, i):
        place = d[5]
        if square:

            @pl.when(place < 2)
            def _():
                hop(d, 0, 2 * i + 1, 1).start()
        else:
            begin(d, 0, 2 * i + 1)

    def begin_pair(d, i):
        begin_even(d, i)
        begin_odd(d, i)

    def begin_rest(d):
        if square:
            tot, place = d[0], d[5]

            @pl.when(place == 0)
            def _():
                @pl.loop(0, pairs)
                def _(i):
                    hop(d, 1, 2 * i + 1, 0, tot.at[0, 2 * i + 1]).start()

    def accept_pair(d, i):
        tot, rcv, _, _, pref, place = d
        accept(d, 2 * i, 0)
        h = 2 * i + 1
        if not square:
            accept(d, h, 0)
            return

        @pl.when(place == 3)
        def _():
            hop(d, 0, h, 1).wait_recv()
            hop(d, 1, h, 0, rcv.at[0, h]).start()
            pref[h] = jnp.exp2(-rate(h, dim) * slab) * rcv[0, h]

        @pl.when(place == 2)
        def _():
            hop(d, 0, h, 1).wait_recv()
            fade = jnp.exp2(-rate(h, dim) * slab)
            got = fade * rcv[0, h]
            tot[1, h] = tot[0, h] + fade * got
            pref[h] = got
            hop(d, 1, h, 0).start()

    def finish_even(d, i):
        if stages > 1:
            accept(d, 2 * i, stages - 1)

    def finish_odd(d, i):
        _, rcv, _, _, pref, place = d
        h = 2 * i + 1
        if square:

            @pl.when(place != 0)
            def _():
                hop(d, 1, h, 0).wait_recv()
                pref[h] = pref[h] + rcv[1, h]
        elif stages > 1:
            accept(d, h, stages - 1)

    def middle(d):
        for s in range(1, stages - 1):

            @pl.loop(0, heads)
            def _(h, s=s):
                accept(d, h, s)

    def settle(d):
        place = d[5]
        for s in range(stages):
            for odd in range(2):
                bit = stages - 1 - s if square and odd else s
                if not (square and odd):
                    cond = sends(s, place)
                elif s == 0:
                    cond = place < 2
                else:
                    cond = place != 1

                @pl.when(cond)
                def _(s=s, odd=odd, bit=bit):
                    @pl.loop(0, pairs)
                    def _(i):
                        hop(d, s, 2 * i + odd, bit).wait_send()

    def local(i):
        falling(2 * i)
        falling(2 * i + 1)
        kv_load(i, 0).wait()
        kv_load(i, 1).wait()
        for odd in range(2):
            h = 2 * i + odd
            faded = (k[:, cols(h)].astype(f32) * down[h]).astype(bf16)
            tot_f[0, h] = dot(faded, v[:, cols(h)], 0, 0)

    local(0)
    for load in loads:
        load.start()
    pl.semaphore_wait(barrier, (stages if square else n_seq - 1) + n_dp - 1 + near_heads)
    first = md == 0

    @pl.when(first)
    def _():
        begin_pair(forward, 0)

    steps = max(n_head - 2, 1)
    greet(ready.at[0])
    if square:
        pl.semaphore_signal(ready.at[0], inc=1, device_id={"seq": partner(0)}, device_id_type=MESH)

    @pl.loop(1, pairs)
    def _(i):
        local(i)

        @pl.when(first)
        def _():
            begin_pair(forward, i)

    @pl.when(first)
    def _():
        begin_rest(forward)

    @pl.loop(0, heads)
    def _(h):
        rising(h)
        pref_f[h] = jnp.zeros((dim, dim), f32)
        pref_b[h] = jnp.zeros((dim, dim), f32)

    loads[0].wait()

    t_at = lax.broadcasted_iota(jnp.int32, (blk, blk), 0)
    s_at = lax.broadcasted_iota(jnp.int32, (blk, blk), 1)
    shift = min(TURN, pairs - 1)

    @pl.loop(0, pairs)
    def _(i):
        for odd in range(2):
            h = 2 * i + odd
            r = rate(h, dim)
            place = lax.broadcasted_iota(jnp.int32, (1, dim), 1).astype(f32)
            front = up[h, pl.ds(0, blk), :]
            near = jnp.concatenate(
                [front * jnp.exp2(r * (place + float(b * dim))) for b in range(blk // dim)],
                axis=1,
            )
            wtab[odd][i, 0] = jnp.where(t_at >= s_at, near, 0.0)
            for d in range(1, nblk):
                away = jnp.exp2(-r * float(blk * d))
                wtab[odd][i, d] = near * jnp.concatenate([away] * (blk // dim), axis=1)
        for a in range(nblk):
            rows = pl.ds(a * blk, blk)
            for odd in range(2):
                h = 2 * i + odd
                for b in range(a + 1):
                    past = pl.ds(b * blk, blk)
                    score = dot(q[rows, cols(h)], k[past, cols(h)], 1, 1)
                    probs[odd][i, rows, past] = (score * wtab[odd][i, a - b]).astype(bf16)
        for a in range(nblk):
            rows = pl.ds(a * blk, blk)
            past = pl.ds(0, (a + 1) * blk)
            for odd in range(2):
                h = 2 * i + odd
                out[rows, cols(h)] = dot(probs[odd][i, rows, past], v[past, cols(h)], 1, 0)

        for ahead in (1, 0):

            @pl.when(jnp.logical_and(first, (2 * i - ahead >= 0) & (2 * i - ahead < pairs)))
            def _(ahead=ahead):
                accept_pair(forward, 2 * i - ahead)

        if n_dp > 1:

            @pl.when(jnp.logical_and(first, i == shift))
            def _():
                pl.semaphore_signal(turn, inc=1, device_id={"dp": 1 - md}, device_id_type=MESH)

            @pl.when(jnp.logical_and(jnp.logical_not(first), i == shift))
            def _():
                pl.semaphore_wait(turn, 1)

                @pl.loop(0, pairs)
                def _(p):
                    begin_pair(forward, p)

                begin_rest(forward)

    @pl.when(jnp.logical_not(first))
    def _():
        @pl.loop(0, pairs)
        def _(i):
            accept_pair(forward, i)

    middle(forward)
    for s in range(steps - 1):
        pl.semaphore_wait(ready.at[s], near_heads + (1 if square and s == 0 else 0))
        greet(ready.at[s + 1])

    loads[1].wait()
    for load in small[1:]:
        load.wait()

    token = mask_ref[...].astype(f32)
    at = me * slab + lax.broadcasted_iota(jnp.int32, (1, slab), 1)
    length = jnp.full((1, slab), len_ref[0], jnp.int32)
    token = token * (at < length).astype(f32) * jnp.minimum(imp_ref[...], clip_high)
    token = token * adv_ref[0] * (float(slab * n_seq) / length.astype(f32))

    squares[...] = jnp.zeros((slab, dim), f32)
    mixes[...] = jnp.zeros((slab, dim), f32)

    def widen(h):
        half = pref_f[h].astype(bf16)
        state[h] = half
        grow = up[h] * jnp.exp2(-rate(h, dim))
        full = out[:, cols(h)] + dot(q[:, cols(h)], half, 1, 0) * grow
        out[:, cols(h)] = full
        return full, c[:, cols(h)].astype(f32) * gain_ref[pl.ds(h, 1), :] * full

    @pl.loop(0, pairs - 1)
    def _(i):
        finish_even(forward, i)
        finish_odd(forward, i)
        full, mix = widen(2 * i)
        other, blend = widen(2 * i + 1)
        squares[...] += full * full + other * other
        mixes[...] += mix + blend

    finish_even(forward, pairs - 1)
    full, mix = widen(heads - 2)
    squares[...] += full * full
    mixes[...] += mix
    finish_odd(forward, pairs - 1)
    full, mix = widen(heads - 1)
    squares[...] += full * full
    mixes[...] += mix

    stat[mh, 0:1, :] = jnp.sum(squares[...].T, axis=0, keepdims=True)
    stat[mh, 1:2, :] = jnp.sum(mixes[...].T, axis=0, keepdims=True) * token
    posts = [
        pltpu.make_async_remote_copy(
            src_ref=stat.at[mh],
            dst_ref=stat.at[mh],
            send_sem=ss_sem.at[off - 1],
            recv_sem=sr_sem.at[off - 1],
            device_id={"head": lax.rem(mh + off, n_head)},
            device_id_type=MESH,
        )
        for off in range(1, n_head)
    ]
    pl.semaphore_wait(ready.at[steps - 1], near_heads + (1 if square and steps == 1 else 0))
    for post in posts:
        post.start()
    for post in posts:
        post.wait_recv()
    sums = stat[0]
    for i in range(1, n_head):
        sums = sums + stat[i]
    count = features * n_head
    inverse = lax.rsqrt(sums[0:1] / count + epsilon)
    mean = inverse * (sums[1:2] / count)

    def column(row):
        return jnp.broadcast_to(row, (dim, slab)).T

    inv_col = column(inverse)
    give_col = column(inverse * token)
    take_col = column(inverse * inverse * mean)

    def give(h):
        given = c[:, cols(h)].astype(f32) * give_col
        grad = (given * gain_ref[pl.ds(h, 1), :] - take_col * out[:, cols(h)]).astype(bf16)
        go[:, cols(h)] = grad
        faded = (q[:, cols(h)].astype(f32) * up[h]).astype(bf16)
        tot_b[0, h] = dot(faded, grad, 0, 0)

    give(0)
    begin_even(backward, 0)
    give(1)
    begin_odd(backward, 0)

    @pl.loop(1, pairs)
    def _(i):
        give(2 * i)
        give(2 * i + 1)
        begin_even(backward, i)
        begin_odd(backward, i)

    begin_rest(backward)

    @pl.loop(0, heads)
    def _(h):
        gain = gain_ref[pl.ds(h, 1), :]
        full = out[:, cols(h)]
        given = c[:, cols(h)].astype(f32) * give_col
        o_mix[0, :, cols(h)] = (full * inv_col * gain).astype(bf16)
        gsum[me, pl.ds(h, 1), :] = jnp.sum(given * full, axis=0, keepdims=True)

    shares = [
        pltpu.make_async_remote_copy(
            src_ref=gsum.at[me],
            dst_ref=gsum.at[me],
            send_sem=gs_sem.at[off],
            recv_sem=gr_sem.at[off],
            device_id={"seq": lax.rem(me + off, n_seq)},
            device_id_type=MESH,
        )
        for off in range(1, n_seq)
    ]
    swap = pltpu.make_async_remote_copy(
        src_ref=gpair.at[0],
        dst_ref=gpair.at[1],
        send_sem=gs_sem.at[0],
        recv_sem=gr_sem.at[0],
        device_id={"dp": lax.rem(md + 1, n_dp)},
        device_id_type=MESH,
    )
    for share in shares:
        share.start()
    late = min(1, pairs - 1)

    @pl.when(first)
    def _():
        accept_pair(backward, 0)

    @pl.loop(0, pairs)
    def _(i):
        for a in range(nblk):
            rows = pl.ds(a * blk, blk)
            for odd in range(2):
                h = 2 * i + odd
                grad = go[rows, cols(h)]
                for b in range(a + 1):
                    past = pl.ds(b * blk, blk)
                    score = dot(grad, v[past, cols(h)], 1, 1)
                    dsc[odd][rows, past] = (score * wtab[odd][i, a - b]).astype(bf16)
        for a in range(nblk):
            rows = pl.ds(a * blk, blk)
            past = pl.ds(0, (a + 1) * blk)
            for odd in range(2):
                h = 2 * i + odd
                grow = up[h, rows, :] * jnp.exp2(-rate(h, dim))
                total = dot(dsc[odd][rows, past], k[past, cols(h)], 1, 0)
                total = total + dot(go[rows, cols(h)], state[h], 1, 1) * grow
                o_dq[0, rows, cols(h)] = total.astype(bf16)
        for b in range(nblk):
            past = pl.ds(b * blk, blk)
            rest = pl.ds(b * blk, slab - b * blk)
            for odd in range(2):
                h = 2 * i + odd
                pk[past, cols(h)] = dot(dsc[odd][rest, past], q[rest, cols(h)], 0, 0)
                pv[past, cols(h)] = dot(probs[odd][i, rest, past], go[rest, cols(h)], 0, 0)

        for ahead in (1, 2):

            @pl.when(jnp.logical_and(first, 2 * i + ahead < pairs))
            def _(ahead=ahead):
                accept_pair(backward, 2 * i + ahead)

        @pl.when(jnp.logical_and(jnp.logical_not(first), i == late))
        def _():
            @pl.loop(0, late)
            def _(p):
                accept_pair(backward, p)

        @pl.when(jnp.logical_and(jnp.logical_not(first), i >= late))
        def _():
            accept_pair(backward, i)

    for share in shares:
        share.wait_recv()
    total = gsum[0]
    for s in range(1, n_seq):
        total = total + gsum[s]
    gpair[0] = total
    if n_dp > 1:
        swap.start()
    middle(backward)

    def close(h):
        half = pref_b[h].astype(bf16)
        fade = down[h] * jnp.exp2(-rate(h, dim))
        dk = pk[:, cols(h)] + dot(v[:, cols(h)], half, 1, 1) * fade
        o_dk[0, :, cols(h)] = dk.astype(bf16)
        dv = pv[:, cols(h)] + dot(k[:, cols(h)], half, 1, 0) * fade
        o_dv[0, :, cols(h)] = dv.astype(bf16)

    @pl.loop(0, pairs - 1)
    def _(i):
        finish_even(backward, i)
        finish_odd(backward, i)
        close(2 * i)
        close(2 * i + 1)

    finish_even(backward, pairs - 1)
    close(heads - 2)
    finish_odd(backward, pairs - 1)
    close(heads - 1)
    if n_dp > 1:
        swap.wait()
        gg_ref[...] = gpair[0] + gpair[1]
    else:
        gg_ref[...] = gpair[0]
    for post in posts + shares:
        post.wait_send()
    settle(forward)
    settle(backward)


def writer(n, *refs):
    sem = refs[-1]
    copies = [pltpu.make_async_copy(refs[i], refs[n + i], sem.at[i]) for i in range(n)]
    for copy in copies:
        copy.start()
    for copy in copies:
        copy.wait()


def on_device(
    n_seq,
    n_head,
    n_dp,
    query_rows,
    key_rows,
    value_rows,
    norm_gain,
    cotangent,
    loss_mask,
    importance,
    advantage,
    lengths,
    decay_index,
):
    batches, slab, features = query_rows.shape
    heads = decay_index.shape[0]
    dim = features // heads
    stages = n_seq.bit_length() - 1
    assert batches == 1 and heads % 2 == 0 and n_seq == 1 << stages and stages > 0 and n_dp <= 2
    vmem = pl.BlockSpec(memory_space=pltpu.VMEM)
    smem = pl.BlockSpec(memory_space=pltpu.SMEM)
    far = pl.BlockSpec(memory_space=pltpu.HBM)
    rows = jax.ShapeDtypeStruct(query_rows.shape, bf16)
    wide = pltpu.VMEM((slab, features), bf16)
    wide32 = pltpu.VMEM((slab, features), f32)
    blk = min(256, slab)
    states = pltpu.VMEM((stages, heads, dim, dim), f32)
    dma = pltpu.SemaphoreType.DMA

    def stay(array):
        return pltpu.with_memory_space_constraint(array, pltpu.HBM)

    results = pl.pallas_call(
        functools.partial(kernel, n_seq, n_head, n_dp),
        out_shape=(rows, rows, rows, rows, jax.ShapeDtypeStruct((heads, dim), f32)),
        in_specs=[far, smem, smem] + [far] * 7,
        out_specs=(vmem,) * 5,
        scratch_shapes=[
            pltpu.SMEM((heads,), jnp.int32),
            pltpu.VMEM((heads, dim), f32),
            pltpu.VMEM((1, slab), jnp.int32),
            pltpu.VMEM((1, slab), f32),
        ]
        + [wide] * 4
        + [wide32, wide, wide32, wide32]
        + [
            pltpu.VMEM((heads // 2, slab, slab), bf16),
            pltpu.VMEM((heads // 2, slab, slab), bf16),
            pltpu.VMEM((slab, slab), bf16),
            pltpu.VMEM((slab, slab), bf16),
            pltpu.VMEM((heads // 2, slab // blk, blk, blk), f32),
            pltpu.VMEM((heads // 2, slab // blk, blk, blk), f32),
            pltpu.VMEM((heads, slab, dim), f32),
            pltpu.VMEM((heads, slab, dim), f32),
            pltpu.VMEM((slab, dim), f32),
            pltpu.VMEM((slab, dim), f32),
            states,
            states,
            states,
            states,
            pltpu.VMEM((heads, dim, dim), f32),
            pltpu.VMEM((heads, dim, dim), f32),
            pltpu.VMEM((heads, dim, dim), bf16),
            pltpu.VMEM((n_head, 2, slab), f32),
            pltpu.VMEM((n_seq, heads, dim), f32),
            pltpu.VMEM((2, heads, dim), f32),
            dma((2,)),
            dma((2, heads // 2)),
            dma((4,)),
            dma((stages, heads)),
            dma((stages, heads)),
            dma((stages, heads)),
            dma((stages, heads)),
            dma((max(n_head - 1, 1),)),
            dma((max(n_head - 1, 1),)),
            dma((n_seq,)),
            dma((n_seq,)),
            pltpu.SemaphoreType.REGULAR,
            pltpu.SemaphoreType.REGULAR((max(n_head - 2, 1),)),
        ],
        compiler_params=pltpu.CompilerParams(
            collective_id=0, has_side_effects=True, vmem_limit_bytes=48 << 20
        ),
        name="lightning",
    )(
        stay(decay_index),
        advantage,
        lengths,
        stay(norm_gain.reshape(heads, dim)),
        stay(loss_mask),
        stay(importance),
        stay(query_rows),
        stay(key_rows),
        stay(value_rows),
        stay(cotangent),
    )
    shapes = tuple(jax.ShapeDtypeStruct(r.shape, r.dtype) for r in results)
    any_space = pl.BlockSpec(memory_space=pl.ANY)
    mixed, dq, dk, dv, gain_grad = pl.pallas_call(
        functools.partial(writer, len(shapes)),
        out_shape=shapes,
        in_specs=[vmem] * len(shapes),
        out_specs=(any_space,) * len(shapes),
        scratch_shapes=[dma((len(shapes),))],
        compiler_params=pltpu.CompilerParams(vmem_limit_bytes=8 << 20),
        name="writer",
    )(*results)
    return (mixed, dq, dk, dv, gain_grad.reshape(features))


def solution(mesh):
    wide = P("dp", "seq", "head")
    token = P("dp", "seq")
    in_specs = (wide, wide, wide, P("head"), wide, token, token, P("dp"), P("dp"), P("head"))
    out_specs = (wide, wide, wide, wide, P("head"))
    body = functools.partial(on_device, mesh.shape["seq"], mesh.shape["head"], mesh.shape["dp"])
    return jax.shard_map(
        body, mesh=mesh, in_specs=in_specs, out_specs=out_specs, check_vma=False
    )
```

```python
import functools

import jax
import jax.numpy as jnp
from jax import lax
from jax.experimental import pallas as pl
from jax.experimental.pallas import tpu as pltpu
from jax.sharding import PartitionSpec as P

clip_high = 1.28
epsilon = 1e-06
f32 = jnp.float32
bf16 = jnp.bfloat16
MESH = pl.DeviceIdType.MESH
TURN = 3


def dot(a, b, ca, cb):
    return lax.dot_general(a, b, (((ca,), (cb,)), ((), ())), preferred_element_type=f32)


def kernel(
    n_seq,
    n_head,
    n_dp,
    decay_hbm,
    adv_ref,
    len_ref,
    gain_hbm,
    mask_hbm,
    imp_hbm,
    q_hbm,
    k_hbm,
    v_hbm,
    c_hbm,
    o_mix,
    o_dq,
    o_dk,
    o_dv,
    gg_ref,
    decay_ref,
    gain_ref,
    mask_ref,
    imp_ref,
    q,
    k,
    v,
    c,
    out,
    go,
    pk,
    pv,
    probs0,
    probs1,
    dsc0,
    dsc1,
    wtab0,
    wtab1,
    up,
    down,
    squares,
    mixes,
    tot_f,
    rcv_f,
    tot_b,
    rcv_b,
    pref_f,
    pref_b,
    state,
    stat,
    gsum,
    gpair,
    in_sem,
    kv_sem,
    small_sem,
    fs_sem,
    fr_sem,
    bs_sem,
    br_sem,
    ss_sem,
    sr_sem,
    gs_sem,
    gr_sem,
    turn,
    ready,
):
    slab, features = q.shape
    heads = decay_ref.shape[0]
    pairs = heads // 2
    dim = features // heads
    blk = min(256, slab)
    nblk = slab // blk
    stages = n_seq.bit_length() - 1
    square = stages == 2
    probs = (probs0, probs1)
    dsc = (dsc0, dsc1)
    wtab = (wtab0, wtab1)
    me = lax.axis_index("seq")
    mh = lax.axis_index("head")
    md = lax.axis_index("dp")
    back = n_seq - 1 - me
    forward = (tot_f, rcv_f, fs_sem, fr_sem, pref_f, me)
    backward = (tot_b, rcv_b, bs_sem, br_sem, pref_b, back)

    def partner(step):
        g = 1 << step
        bit = lax.rem(lax.div(me, g), 2)
        return me + g * (1 - 2 * bit)

    def kv_load(i, which):
        src, dst = ((k_hbm, k), (v_hbm, v))[which]
        span = pl.ds(pl.multiple_of(i * 2 * dim, 2 * dim), 2 * dim)
        return pltpu.make_async_copy(src.at[0, :, span], dst.at[:, span], kv_sem.at[which, i])

    loads = [
        pltpu.make_async_copy(src.at[0], dst, in_sem.at[i])
        for i, (src, dst) in enumerate(((q_hbm, q), (c_hbm, c)))
    ]
    small = [
        pltpu.make_async_copy(src, dst, small_sem.at[i])
        for i, (src, dst) in enumerate(
            (
                (decay_hbm, decay_ref),
                (gain_hbm, gain_ref),
                (mask_hbm, mask_ref),
                (imp_hbm, imp_ref),
            )
        )
    ]
    barrier = pltpu.get_barrier_semaphore()
    if square:
        for s in range(stages):
            pl.semaphore_signal(barrier, inc=1, device_id={"seq": partner(s)}, device_id_type=MESH)
    else:
        for off in range(1, n_seq):
            pl.semaphore_signal(
                barrier, inc=1, device_id={"seq": lax.rem(me + off, n_seq)}, device_id_type=MESH
            )
    near_heads = (mh > 0).astype(jnp.int32) + (mh < n_head - 1).astype(jnp.int32)

    def greet(sem):
        @pl.when(mh > 0)
        def _():
            pl.semaphore_signal(sem, inc=1, device_id={"head": mh - 1}, device_id_type=MESH)

        @pl.when(mh < n_head - 1)
        def _():
            pl.semaphore_signal(sem, inc=1, device_id={"head": mh + 1}, device_id_type=MESH)

    greet(barrier)
    small[0].start()
    kv_load(0, 0).start()
    kv_load(0, 1).start()
    for off in range(1, n_dp):
        pl.semaphore_signal(
            barrier, inc=1, device_id={"dp": lax.rem(md + off, n_dp)}, device_id_type=MESH
        )

    for i in range(1, pairs):
        kv_load(i, 0).start()
        kv_load(i, 1).start()
    for load in small[1:]:
        load.start()

    def cols(h):
        return pl.ds(pl.multiple_of(h * dim, dim), dim)

    def rate(h, width):
        index = jnp.full((1, width), decay_ref[h], jnp.int32).astype(f32)
        return 16.0 / (slab * jnp.exp2(index))

    small[0].wait()
    base = min(128, slab)
    line = lax.broadcasted_iota(jnp.int32, (base, dim), 0).astype(f32)

    def falling(h):
        r = rate(h, dim)
        fall = jnp.exp2(-r * (base - 1.0 - line))
        for b in range(slab // base):
            rows = pl.ds(b * base, base)
            down[h, rows, :] = fall * jnp.exp2(-r * float(slab - (b + 1) * base))

    def rising(h):
        r = rate(h, dim)
        rise = jnp.exp2(-r * line)
        for b in range(slab // base):
            rows = pl.ds(b * base, base)
            up[h, rows, :] = rise * jnp.exp2(-r * float(b * base))

    def hop(d, s, h, bit, src=None):
        tot, rcv, send, recv, _, _ = d
        return pltpu.make_async_remote_copy(
            src_ref=tot.at[s, h] if src is None else src,
            dst_ref=rcv.at[s, h],
            send_sem=send.at[s, h],
            recv_sem=recv.at[s, h],
            device_id={"seq": partner(bit)},
            device_id_type=MESH,
        )

    def lower_only(s, place):
        return lax.div(place, 2 << s) == n_seq // (2 << s) - 1

    def is_upper(s, place):
        return lax.rem(lax.div(place, 1 << s), 2) == 1

    def sends(s, place):
        return jnp.logical_not(jnp.logical_and(is_upper(s, place), lower_only(s, place)))

    def takes(s, place):
        return jnp.logical_or(is_upper(s, place), jnp.logical_not(lower_only(s, place)))

    def begin(d, s, h):
        @pl.when(sends(s, d[5]))
        def _():
            hop(d, s, h, s).start()

    def accept(d, h, s):
        tot, rcv, _, _, pref, place = d

        @pl.when(takes(s, place))
        def _():
            hop(d, s, h, s).wait_recv()
            g = 1 << s
            r = rate(h, dim) * slab
            upper = jnp.full((1, dim), lax.rem(lax.div(place, g), 2), jnp.int32).astype(f32)
            inner = jnp.full((1, dim), lax.rem(place, g), jnp.int32).astype(f32)
            got = rcv[s, h]
            to_prefix = upper * jnp.exp2(-r * inner)
            if s == 0:
                pref[h] = to_prefix * got
            else:
                pref[h] = pref[h] + to_prefix * got
            if s + 1 < stages:
                whole = jnp.exp2(-r * g)
                from_got = upper * whole + (1.0 - upper)
                from_own = upper + (1.0 - upper) * whole
                tot[s + 1, h] = from_got * got + from_own * tot[s, h]

        if s + 1 < stages:
            begin(d, s + 1, h)

    def begin_even(d, i):
        begin(d, 0, 2 * i)

    def begin_odd(d, i):
        place = d[5]
        if square:

            @pl.when(place < 2)
            def _():
                hop(d, 0, 2 * i + 1, 1).start()
        else:
            begin(d, 0, 2 * i + 1)

    def begin_pair(d, i):
        begin_even(d, i)
        begin_odd(d, i)

    def begin_rest(d):
        if square:
            tot, place = d[0], d[5]

            @pl.when(place == 0)
            def _():
                @pl.loop(0, pairs)
                def _(i):
                    hop(d, 1, 2 * i + 1, 0, tot.at[0, 2 * i + 1]).start()

    def accept_pair(d, i):
        tot, rcv, _, _, pref, place = d
        accept(d, 2 * i, 0)
        h = 2 * i + 1
        if not square:
            accept(d, h, 0)
            return

        @pl.when(place == 3)
        def _():
            hop(d, 0, h, 1).wait_recv()
            hop(d, 1, h, 0, rcv.at[0, h]).start()
            pref[h] = jnp.exp2(-rate(h, dim) * slab) * rcv[0, h]

        @pl.when(place == 2)
        def _():
            hop(d, 0, h, 1).wait_recv()
            fade = jnp.exp2(-rate(h, dim) * slab)
            got = fade * rcv[0, h]
            tot[1, h] = tot[0, h] + fade * got
            pref[h] = got
            hop(d, 1, h, 0).start()

    def finish_even(d, i):
        if stages > 1:
            accept(d, 2 * i, stages - 1)

    def finish_odd(d, i):
        _, rcv, _, _, pref, place = d
        h = 2 * i + 1
        if square:

            @pl.when(place != 0)
            def _():
                hop(d, 1, h, 0).wait_recv()
                pref[h] = pref[h] + rcv[1, h]
        elif stages > 1:
            accept(d, h, stages - 1)

    def middle(d):
        for s in range(1, stages - 1):

            @pl.loop(0, heads)
            def _(h, s=s):
                accept(d, h, s)

    def settle(d, which):
        place = d[5]
        for s in which:
            for odd in range(2):
                bit = stages - 1 - s if square and odd else s
                if not (square and odd):
                    cond = sends(s, place)
                elif s == 0:
                    cond = place < 2
                else:
                    cond = place != 1

                @pl.when(cond)
                def _(s=s, odd=odd, bit=bit):
                    @pl.loop(0, pairs)
                    def _(i):
                        hop(d, s, 2 * i + odd, bit).wait_send()

    def local(i):
        falling(2 * i)
        falling(2 * i + 1)
        kv_load(i, 0).wait()
        kv_load(i, 1).wait()
        for odd in range(2):
            h = 2 * i + odd
            faded = (k[:, cols(h)].astype(f32) * down[h]).astype(bf16)
            tot_f[0, h] = dot(faded, v[:, cols(h)], 0, 0)

    local(0)
    for load in loads:
        load.start()
    pl.semaphore_wait(barrier, (stages if square else n_seq - 1) + n_dp - 1 + near_heads)
    first = md == 0

    @pl.when(first)
    def _():
        begin_pair(forward, 0)

    steps = max(n_head - 2, 1)
    greet(ready.at[0])
    if square:
        pl.semaphore_signal(ready.at[0], inc=1, device_id={"seq": partner(0)}, device_id_type=MESH)

    @pl.loop(1, pairs)
    def _(i):
        local(i)

        @pl.when(first)
        def _():
            begin_pair(forward, i)

    @pl.when(first)
    def _():
        begin_rest(forward)

    @pl.loop(0, heads)
    def _(h):
        rising(h)
        pref_f[h] = jnp.zeros((dim, dim), f32)
        pref_b[h] = jnp.zeros((dim, dim), f32)

    loads[0].wait()

    t_at = lax.broadcasted_iota(jnp.int32, (blk, blk), 0)
    s_at = lax.broadcasted_iota(jnp.int32, (blk, blk), 1)
    shift = min(TURN, pairs - 1)

    @pl.loop(0, pairs)
    def _(i):
        for odd in range(2):
            h = 2 * i + odd
            r = rate(h, dim)
            place = lax.broadcasted_iota(jnp.int32, (1, dim), 1).astype(f32)
            front = up[h, pl.ds(0, blk), :]
            near = jnp.concatenate(
                [front * jnp.exp2(r * (place + float(b * dim))) for b in range(blk // dim)],
                axis=1,
            )
            wtab[odd][i, 0] = jnp.where(t_at >= s_at, near, 0.0)
            for d in range(1, nblk):
                away = jnp.exp2(-r * float(blk * d))
                wtab[odd][i, d] = near * jnp.concatenate([away] * (blk // dim), axis=1)
        for a in range(nblk):
            rows = pl.ds(a * blk, blk)
            for odd in range(2):
                h = 2 * i + odd
                for b in range(a + 1):
                    past = pl.ds(b * blk, blk)
                    score = dot(q[rows, cols(h)], k[past, cols(h)], 1, 1)
                    probs[odd][i, rows, past] = (score * wtab[odd][i, a - b]).astype(bf16)
        for a in range(nblk):
            rows = pl.ds(a * blk, blk)
            past = pl.ds(0, (a + 1) * blk)
            for odd in range(2):
                h = 2 * i + odd
                out[rows, cols(h)] = dot(probs[odd][i, rows, past], v[past, cols(h)], 1, 0)

        for ahead in (1, 0):

            @pl.when(jnp.logical_and(first, (2 * i - ahead >= 0) & (2 * i - ahead < pairs)))
            def _(ahead=ahead):
                accept_pair(forward, 2 * i - ahead)

        if n_dp > 1:

            @pl.when(jnp.logical_and(first, i == shift))
            def _():
                pl.semaphore_signal(turn, inc=1, device_id={"dp": 1 - md}, device_id_type=MESH)

            @pl.when(jnp.logical_and(jnp.logical_not(first), i == shift))
            def _():
                pl.semaphore_wait(turn, 1)

                @pl.loop(0, pairs)
                def _(p):
                    begin_pair(forward, p)

                begin_rest(forward)

    @pl.when(jnp.logical_not(first))
    def _():
        @pl.loop(0, pairs)
        def _(i):
            accept_pair(forward, i)

    middle(forward)
    for s in range(steps - 1):
        pl.semaphore_wait(ready.at[s], near_heads + (1 if square and s == 0 else 0))
        greet(ready.at[s + 1])

    loads[1].wait()
    for load in small[1:]:
        load.wait()

    token = mask_ref[...].astype(f32)
    at = me * slab + lax.broadcasted_iota(jnp.int32, (1, slab), 1)
    length = jnp.full((1, slab), len_ref[0], jnp.int32)
    token = token * (at < length).astype(f32) * jnp.minimum(imp_ref[...], clip_high)
    token = token * adv_ref[0] * (float(slab * n_seq) / length.astype(f32))

    squares[...] = jnp.zeros((slab, dim), f32)
    mixes[...] = jnp.zeros((slab, dim), f32)

    def widen(h):
        half = pref_f[h].astype(bf16)
        state[h] = half
        grow = up[h] * jnp.exp2(-rate(h, dim))
        full = out[:, cols(h)] + dot(q[:, cols(h)], half, 1, 0) * grow
        out[:, cols(h)] = full
        return full, c[:, cols(h)].astype(f32) * gain_ref[pl.ds(h, 1), :] * full

    @pl.loop(0, pairs - 1)
    def _(i):
        finish_even(forward, i)
        finish_odd(forward, i)
        full, mix = widen(2 * i)
        other, blend = widen(2 * i + 1)
        squares[...] += full * full + other * other
        mixes[...] += mix + blend

    finish_even(forward, pairs - 1)
    full, mix = widen(heads - 2)
    squares[...] += full * full
    mixes[...] += mix
    finish_odd(forward, pairs - 1)
    full, mix = widen(heads - 1)
    squares[...] += full * full
    mixes[...] += mix

    stat[mh, 0:1, :] = jnp.sum(squares[...].T, axis=0, keepdims=True)
    stat[mh, 1:2, :] = jnp.sum(mixes[...].T, axis=0, keepdims=True) * token
    posts = [
        pltpu.make_async_remote_copy(
            src_ref=stat.at[mh],
            dst_ref=stat.at[mh],
            send_sem=ss_sem.at[off - 1],
            recv_sem=sr_sem.at[off - 1],
            device_id={"head": lax.rem(mh + off, n_head)},
            device_id_type=MESH,
        )
        for off in range(1, n_head)
    ]
    pl.semaphore_wait(ready.at[steps - 1], near_heads + (1 if square and steps == 1 else 0))
    for post in posts:
        post.start()
    for post in posts:
        post.wait_recv()
    sums = stat[0]
    for i in range(1, n_head):
        sums = sums + stat[i]
    count = features * n_head
    inverse = lax.rsqrt(sums[0:1] / count + epsilon)
    mean = inverse * (sums[1:2] / count)

    def column(row):
        return jnp.broadcast_to(row, (dim, slab)).T

    inv_col = column(inverse)
    give_col = column(inverse * token)
    take_col = column(inverse * inverse * mean)

    def give(h):
        given = c[:, cols(h)].astype(f32) * give_col
        grad = (given * gain_ref[pl.ds(h, 1), :] - take_col * out[:, cols(h)]).astype(bf16)
        go[:, cols(h)] = grad
        faded = (q[:, cols(h)].astype(f32) * up[h]).astype(bf16)
        tot_b[0, h] = dot(faded, grad, 0, 0)

    give(0)
    begin_even(backward, 0)
    give(1)
    begin_odd(backward, 0)

    @pl.loop(1, pairs)
    def _(i):
        give(2 * i)
        give(2 * i + 1)
        begin_even(backward, i)
        begin_odd(backward, i)

    begin_rest(backward)

    @pl.loop(0, heads)
    def _(h):
        gain = gain_ref[pl.ds(h, 1), :]
        full = out[:, cols(h)]
        given = c[:, cols(h)].astype(f32) * give_col
        o_mix[0, :, cols(h)] = (full * inv_col * gain).astype(bf16)
        gsum[me, pl.ds(h, 1), :] = jnp.sum(given * full, axis=0, keepdims=True)

    shares = [
        pltpu.make_async_remote_copy(
            src_ref=gsum.at[me],
            dst_ref=gsum.at[me],
            send_sem=gs_sem.at[off],
            recv_sem=gr_sem.at[off],
            device_id={"seq": lax.rem(me + off, n_seq)},
            device_id_type=MESH,
        )
        for off in range(1, n_seq)
    ]
    swap = pltpu.make_async_remote_copy(
        src_ref=gpair.at[0],
        dst_ref=gpair.at[1],
        send_sem=gs_sem.at[0],
        recv_sem=gr_sem.at[0],
        device_id={"dp": lax.rem(md + 1, n_dp)},
        device_id_type=MESH,
    )
    for share in shares:
        share.start()
    late = min(1, pairs - 1)

    @pl.when(first)
    def _():
        @pl.loop(0, min(2, pairs))
        def _(i):
            accept_pair(backward, i)

    @pl.loop(0, pairs)
    def _(i):
        for a in range(nblk):
            rows = pl.ds(a * blk, blk)
            for odd in range(2):
                h = 2 * i + odd
                grad = go[rows, cols(h)]
                for b in range(a + 1):
                    past = pl.ds(b * blk, blk)
                    score = dot(grad, v[past, cols(h)], 1, 1)
                    dsc[odd][rows, past] = (score * wtab[odd][i, a - b]).astype(bf16)
        for a in range(nblk):
            rows = pl.ds(a * blk, blk)
            past = pl.ds(0, (a + 1) * blk)
            for odd in range(2):
                h = 2 * i + odd
                grow = up[h, rows, :] * jnp.exp2(-rate(h, dim))
                total = dot(dsc[odd][rows, past], k[past, cols(h)], 1, 0)
                total = total + dot(go[rows, cols(h)], state[h], 1, 1) * grow
                o_dq[0, rows, cols(h)] = total.astype(bf16)
        for b in range(nblk):
            past = pl.ds(b * blk, blk)
            rest = pl.ds(b * blk, slab - b * blk)
            for odd in range(2):
                h = 2 * i + odd
                pk[past, cols(h)] = dot(dsc[odd][rest, past], q[rest, cols(h)], 0, 0)
                pv[past, cols(h)] = dot(probs[odd][i, rest, past], go[rest, cols(h)], 0, 0)

        for ahead in (2, 3):

            @pl.when(jnp.logical_and(first, 2 * i + ahead < pairs))
            def _(ahead=ahead):
                accept_pair(backward, 2 * i + ahead)

        @pl.when(jnp.logical_and(jnp.logical_not(first), i == late))
        def _():
            @pl.loop(0, late)
            def _(p):
                accept_pair(backward, p)

        @pl.when(jnp.logical_and(jnp.logical_not(first), i >= late))
        def _():
            accept_pair(backward, i)

    for share in shares:
        share.wait_recv()
    total = gsum[0]
    for s in range(1, n_seq):
        total = total + gsum[s]
    gpair[0] = total
    if n_dp > 1:
        swap.start()
    middle(backward)

    def close(h):
        half = pref_b[h].astype(bf16)
        fade = down[h] * jnp.exp2(-rate(h, dim))
        dk = pk[:, cols(h)] + dot(v[:, cols(h)], half, 1, 1) * fade
        o_dk[0, :, cols(h)] = dk.astype(bf16)
        dv = pv[:, cols(h)] + dot(k[:, cols(h)], half, 1, 0) * fade
        o_dv[0, :, cols(h)] = dv.astype(bf16)

    @pl.loop(0, pairs - 1)
    def _(i):
        finish_even(backward, i)
        finish_odd(backward, i)
        close(2 * i)
        close(2 * i + 1)

    for post in posts + shares:
        post.wait_send()
    settle(forward, range(stages))
    settle(backward, range(stages - 1))
    finish_even(backward, pairs - 1)
    close(heads - 2)
    finish_odd(backward, pairs - 1)
    close(heads - 1)
    if n_dp > 1:
        swap.wait()
        gg_ref[...] = gpair[0] + gpair[1]
    else:
        gg_ref[...] = gpair[0]
    settle(backward, range(stages - 1, stages))


def writer(n, *refs):
    sem = refs[-1]
    copies = [pltpu.make_async_copy(refs[i], refs[n + i], sem.at[i]) for i in range(n)]
    for copy in copies:
        copy.start()
    for copy in copies:
        copy.wait()


def on_device(
    n_seq,
    n_head,
    n_dp,
    query_rows,
    key_rows,
    value_rows,
    norm_gain,
    cotangent,
    loss_mask,
    importance,
    advantage,
    lengths,
    decay_index,
):
    batches, slab, features = query_rows.shape
    heads = decay_index.shape[0]
    dim = features // heads
    stages = n_seq.bit_length() - 1
    assert batches == 1 and heads % 2 == 0 and n_seq == 1 << stages and stages > 0 and n_dp <= 2
    vmem = pl.BlockSpec(memory_space=pltpu.VMEM)
    smem = pl.BlockSpec(memory_space=pltpu.SMEM)
    far = pl.BlockSpec(memory_space=pltpu.HBM)
    rows = jax.ShapeDtypeStruct(query_rows.shape, bf16)
    wide = pltpu.VMEM((slab, features), bf16)
    wide32 = pltpu.VMEM((slab, features), f32)
    blk = min(256, slab)
    states = pltpu.VMEM((stages, heads, dim, dim), f32)
    dma = pltpu.SemaphoreType.DMA

    def stay(array):
        return pltpu.with_memory_space_constraint(array, pltpu.HBM)

    results = pl.pallas_call(
        functools.partial(kernel, n_seq, n_head, n_dp),
        out_shape=(rows, rows, rows, rows, jax.ShapeDtypeStruct((heads, dim), f32)),
        in_specs=[far, smem, smem] + [far] * 7,
        out_specs=(vmem,) * 5,
        scratch_shapes=[
            pltpu.SMEM((heads,), jnp.int32),
            pltpu.VMEM((heads, dim), f32),
            pltpu.VMEM((1, slab), jnp.int32),
            pltpu.VMEM((1, slab), f32),
        ]
        + [wide] * 4
        + [wide32, wide, wide32, wide32]
        + [
            pltpu.VMEM((heads // 2, slab, slab), bf16),
            pltpu.VMEM((heads // 2, slab, slab), bf16),
            pltpu.VMEM((slab, slab), bf16),
            pltpu.VMEM((slab, slab), bf16),
            pltpu.VMEM((heads // 2, slab // blk, blk, blk), f32),
            pltpu.VMEM((heads // 2, slab // blk, blk, blk), f32),
            pltpu.VMEM((heads, slab, dim), f32),
            pltpu.VMEM((heads, slab, dim), f32),
            pltpu.VMEM((slab, dim), f32),
            pltpu.VMEM((slab, dim), f32),
            states,
            states,
            states,
            states,
            pltpu.VMEM((heads, dim, dim), f32),
            pltpu.VMEM((heads, dim, dim), f32),
            pltpu.VMEM((heads, dim, dim), bf16),
            pltpu.VMEM((n_head, 2, slab), f32),
            pltpu.VMEM((n_seq, heads, dim), f32),
            pltpu.VMEM((2, heads, dim), f32),
            dma((2,)),
            dma((2, heads // 2)),
            dma((4,)),
            dma((stages, heads)),
            dma((stages, heads)),
            dma((stages, heads)),
            dma((stages, heads)),
            dma((max(n_head - 1, 1),)),
            dma((max(n_head - 1, 1),)),
            dma((n_seq,)),
            dma((n_seq,)),
            pltpu.SemaphoreType.REGULAR,
            pltpu.SemaphoreType.REGULAR((max(n_head - 2, 1),)),
        ],
        compiler_params=pltpu.CompilerParams(
            collective_id=0, has_side_effects=True, vmem_limit_bytes=48 << 20
        ),
        name="lightning",
    )(
        stay(decay_index),
        advantage,
        lengths,
        stay(norm_gain.reshape(heads, dim)),
        stay(loss_mask),
        stay(importance),
        stay(query_rows),
        stay(key_rows),
        stay(value_rows),
        stay(cotangent),
    )
    shapes = tuple(jax.ShapeDtypeStruct(r.shape, r.dtype) for r in results)
    any_space = pl.BlockSpec(memory_space=pl.ANY)
    mixed, dq, dk, dv, gain_grad = pl.pallas_call(
        functools.partial(writer, len(shapes)),
        out_shape=shapes,
        in_specs=[vmem] * len(shapes),
        out_specs=(any_space,) * len(shapes),
        scratch_shapes=[dma((len(shapes),))],
        compiler_params=pltpu.CompilerParams(vmem_limit_bytes=8 << 20),
        name="writer",
    )(*results)
    return (mixed, dq, dk, dv, gain_grad.reshape(features))


def solution(mesh):
    wide = P("dp", "seq", "head")
    token = P("dp", "seq")
    in_specs = (wide, wide, wide, P("head"), wide, token, token, P("dp"), P("dp"), P("head"))
    out_specs = (wide, wide, wide, wide, P("head"))
    body = functools.partial(on_device, mesh.shape["seq"], mesh.shape["head"], mesh.shape["dp"])
    return jax.shard_map(
        body, mesh=mesh, in_specs=in_specs, out_specs=out_specs, check_vma=False
    )
```

```python
import functools

import jax
import jax.numpy as jnp
from jax import lax
from jax.experimental import pallas as pl
from jax.experimental.pallas import tpu as pltpu
from jax.sharding import PartitionSpec as P

clip_high = 1.28
epsilon = 1e-06
f32 = jnp.float32
bf16 = jnp.bfloat16
MESH = pl.DeviceIdType.MESH
TURN = 6


def dot(a, b, ca, cb):
    return lax.dot_general(a, b, (((ca,), (cb,)), ((), ())), preferred_element_type=f32)


def kernel(
    n_seq,
    n_head,
    n_dp,
    decay_hbm,
    adv_ref,
    len_ref,
    gain_hbm,
    mask_hbm,
    imp_hbm,
    q_hbm,
    k_hbm,
    v_hbm,
    c_hbm,
    o_mix,
    o_dq,
    o_dk,
    o_dv,
    gg_ref,
    decay_ref,
    gain_ref,
    mask_ref,
    imp_ref,
    q,
    k,
    v,
    c,
    out,
    go,
    pk,
    pv,
    probs0,
    probs1,
    dsc0,
    dsc1,
    wtab0,
    wtab1,
    up,
    down,
    squares,
    mixes,
    tot_f,
    rcv_f,
    tot_b,
    rcv_b,
    pref_f,
    pref_b,
    state,
    stat,
    gsum,
    gpair,
    in_sem,
    kv_sem,
    small_sem,
    fs_sem,
    fr_sem,
    bs_sem,
    br_sem,
    ss_sem,
    sr_sem,
    gs_sem,
    gr_sem,
    turn,
    ready,
):
    slab, features = q.shape
    heads = decay_ref.shape[0]
    pairs = heads // 2
    dim = features // heads
    blk = min(256, slab)
    nblk = slab // blk
    stages = n_seq.bit_length() - 1
    square = stages == 2
    probs = (probs0, probs1)
    dsc = (dsc0, dsc1)
    wtab = (wtab0, wtab1)
    me = lax.axis_index("seq")
    mh = lax.axis_index("head")
    md = lax.axis_index("dp")
    back = n_seq - 1 - me
    forward = (tot_f, rcv_f, fs_sem, fr_sem, pref_f, me)
    backward = (tot_b, rcv_b, bs_sem, br_sem, pref_b, back)

    def partner(step):
        g = 1 << step
        bit = lax.rem(lax.div(me, g), 2)
        return me + g * (1 - 2 * bit)

    def kv_load(i, which):
        src, dst = ((k_hbm, k), (v_hbm, v))[which]
        span = pl.ds(pl.multiple_of(i * 2 * dim, 2 * dim), 2 * dim)
        return pltpu.make_async_copy(src.at[0, :, span], dst.at[:, span], kv_sem.at[which, i])

    loads = [
        pltpu.make_async_copy(src.at[0], dst, in_sem.at[i])
        for i, (src, dst) in enumerate(((q_hbm, q), (c_hbm, c)))
    ]
    small = [
        pltpu.make_async_copy(src, dst, small_sem.at[i])
        for i, (src, dst) in enumerate(
            (
                (decay_hbm, decay_ref),
                (gain_hbm, gain_ref),
                (mask_hbm, mask_ref),
                (imp_hbm, imp_ref),
            )
        )
    ]
    small[0].start()
    kv_load(0, 0).start()
    kv_load(0, 1).start()

    barrier = pltpu.get_barrier_semaphore()
    if square:
        for s in range(stages):
            pl.semaphore_signal(barrier, inc=1, device_id={"seq": partner(s)}, device_id_type=MESH)
    else:
        for off in range(1, n_seq):
            pl.semaphore_signal(
                barrier, inc=1, device_id={"seq": lax.rem(me + off, n_seq)}, device_id_type=MESH
            )
    near_heads = (mh > 0).astype(jnp.int32) + (mh < n_head - 1).astype(jnp.int32)

    def greet(sem):
        @pl.when(mh > 0)
        def _():
            pl.semaphore_signal(sem, inc=1, device_id={"head": mh - 1}, device_id_type=MESH)

        @pl.when(mh < n_head - 1)
        def _():
            pl.semaphore_signal(sem, inc=1, device_id={"head": mh + 1}, device_id_type=MESH)

    greet(barrier)
    for off in range(1, n_dp):
        pl.semaphore_signal(
            barrier, inc=1, device_id={"dp": lax.rem(md + off, n_dp)}, device_id_type=MESH
        )

    for i in range(1, pairs):
        kv_load(i, 0).start()
        kv_load(i, 1).start()
    for load in small[1:]:
        load.start()

    def cols(h):
        return pl.ds(pl.multiple_of(h * dim, dim), dim)

    def rate(h, width):
        index = jnp.full((1, width), decay_ref[h], jnp.int32).astype(f32)
        return 16.0 / (slab * jnp.exp2(index))

    small[0].wait()
    base = min(128, slab)
    line = lax.broadcasted_iota(jnp.int32, (base, dim), 0).astype(f32)

    def falling(h):
        r = rate(h, dim)
        fall = jnp.exp2(-r * (base - 1.0 - line))
        for b in range(slab // base):
            rows = pl.ds(b * base, base)
            down[h, rows, :] = fall * jnp.exp2(-r * float(slab - (b + 1) * base))

    def rising(h):
        r = rate(h, dim)
        rise = jnp.exp2(-r * line)
        for b in range(slab // base):
            rows = pl.ds(b * base, base)
            up[h, rows, :] = rise * jnp.exp2(-r * float(b * base))

    def hop(d, s, h, bit, src=None):
        tot, rcv, send, recv, _, _ = d
        return pltpu.make_async_remote_copy(
            src_ref=tot.at[s, h] if src is None else src,
            dst_ref=rcv.at[s, h],
            send_sem=send.at[s, h],
            recv_sem=recv.at[s, h],
            device_id={"seq": partner(bit)},
            device_id_type=MESH,
        )

    def lower_only(s, place):
        return lax.div(place, 2 << s) == n_seq // (2 << s) - 1

    def is_upper(s, place):
        return lax.rem(lax.div(place, 1 << s), 2) == 1

    def sends(s, place):
        return jnp.logical_not(jnp.logical_and(is_upper(s, place), lower_only(s, place)))

    def takes(s, place):
        return jnp.logical_or(is_upper(s, place), jnp.logical_not(lower_only(s, place)))

    def begin(d, s, h):
        @pl.when(sends(s, d[5]))
        def _():
            hop(d, s, h, s).start()

    def accept(d, h, s):
        tot, rcv, _, _, pref, place = d

        @pl.when(takes(s, place))
        def _():
            hop(d, s, h, s).wait_recv()
            g = 1 << s
            r = rate(h, dim) * slab
            upper = jnp.full((1, dim), lax.rem(lax.div(place, g), 2), jnp.int32).astype(f32)
            inner = jnp.full((1, dim), lax.rem(place, g), jnp.int32).astype(f32)
            got = rcv[s, h]
            to_prefix = upper * jnp.exp2(-r * inner)
            if s == 0:
                pref[h] = to_prefix * got
            else:
                pref[h] = pref[h] + to_prefix * got
            if s + 1 < stages:
                whole = jnp.exp2(-r * g)
                from_got = upper * whole + (1.0 - upper)
                from_own = upper + (1.0 - upper) * whole
                tot[s + 1, h] = from_got * got + from_own * tot[s, h]

        if s + 1 < stages:
            begin(d, s + 1, h)

    def begin_even(d, i):
        begin(d, 0, 2 * i)

    def begin_odd(d, i):
        place = d[5]
        if square:

            @pl.when(place < 2)
            def _():
                hop(d, 0, 2 * i + 1, 1).start()
        else:
            begin(d, 0, 2 * i + 1)

    def begin_pair(d, i):
        begin_even(d, i)
        begin_odd(d, i)

    def begin_rest(d):
        if square:
            tot, place = d[0], d[5]

            @pl.when(place == 0)
            def _():
                @pl.loop(0, pairs)
                def _(i):
                    hop(d, 1, 2 * i + 1, 0, tot.at[0, 2 * i + 1]).start()

    def accept_pair(d, i):
        tot, rcv, _, _, pref, place = d
        accept(d, 2 * i, 0)
        h = 2 * i + 1
        if not square:
            accept(d, h, 0)
            return

        @pl.when(place == 3)
        def _():
            hop(d, 0, h, 1).wait_recv()
            hop(d, 1, h, 0, rcv.at[0, h]).start()
            pref[h] = jnp.exp2(-rate(h, dim) * slab) * rcv[0, h]

        @pl.when(place == 2)
        def _():
            hop(d, 0, h, 1).wait_recv()
            fade = jnp.exp2(-rate(h, dim) * slab)
            got = fade * rcv[0, h]
            tot[1, h] = tot[0, h] + fade * got
            pref[h] = got
            hop(d, 1, h, 0).start()

    def finish_even(d, i):
        if stages > 1:
            accept(d, 2 * i, stages - 1)

    def finish_odd(d, i):
        _, rcv, _, _, pref, place = d
        h = 2 * i + 1
        if square:

            @pl.when(place != 0)
            def _():
                hop(d, 1, h, 0).wait_recv()
                pref[h] = pref[h] + rcv[1, h]
        elif stages > 1:
            accept(d, h, stages - 1)

    def middle(d):
        for s in range(1, stages - 1):

            @pl.loop(0, heads)
            def _(h, s=s):
                accept(d, h, s)

    def settle(d):
        place = d[5]
        for s in range(stages):
            for odd in range(2):
                bit = stages - 1 - s if square and odd else s
                if not (square and odd):
                    cond = sends(s, place)
                elif s == 0:
                    cond = place < 2
                else:
                    cond = place != 1

                @pl.when(cond)
                def _(s=s, odd=odd, bit=bit):
                    @pl.loop(0, pairs)
                    def _(i):
                        hop(d, s, 2 * i + odd, bit).wait_send()

    def local(i):
        falling(2 * i)
        falling(2 * i + 1)
        kv_load(i, 0).wait()
        kv_load(i, 1).wait()
        for odd in range(2):
            h = 2 * i + odd
            faded = (k[:, cols(h)].astype(f32) * down[h]).astype(bf16)
            tot_f[0, h] = dot(faded, v[:, cols(h)], 0, 0)

    local(0)
    for load in loads:
        load.start()
    pl.semaphore_wait(barrier, (stages if square else n_seq - 1) + n_dp - 1 + near_heads)
    first = md == 0

    @pl.when(first)
    def _():
        begin_pair(forward, 0)

    steps = max(n_head - 2, 1)
    greet(ready.at[0])
    if square:
        pl.semaphore_signal(ready.at[0], inc=1, device_id={"seq": partner(0)}, device_id_type=MESH)

    @pl.loop(1, pairs)
    def _(i):
        local(i)

        @pl.when(first)
        def _():
            begin_pair(forward, i)

    @pl.when(first)
    def _():
        begin_rest(forward)

    @pl.loop(0, heads)
    def _(h):
        rising(h)
        pref_f[h] = jnp.zeros((dim, dim), f32)
        pref_b[h] = jnp.zeros((dim, dim), f32)

    loads[0].wait()

    t_at = lax.broadcasted_iota(jnp.int32, (blk, blk), 0)
    s_at = lax.broadcasted_iota(jnp.int32, (blk, blk), 1)
    shift = min(TURN, heads - 1)

    def attend(h, odd, i):
        r = rate(h, dim)
        place = lax.broadcasted_iota(jnp.int32, (1, dim), 1).astype(f32)
        front = up[h, pl.ds(0, blk), :]
        near = jnp.concatenate(
            [front * jnp.exp2(r * (place + float(b * dim))) for b in range(blk // dim)], axis=1
        )
        wtab[odd][i, 0] = jnp.where(t_at >= s_at, near, 0.0)
        for d in range(1, nblk):
            away = jnp.exp2(-r * float(blk * d))
            wtab[odd][i, d] = near * jnp.concatenate([away] * (blk // dim), axis=1)
        for a in range(nblk):
            rows = pl.ds(a * blk, blk)
            for b in range(a + 1):
                past = pl.ds(b * blk, blk)
                score = dot(q[rows, cols(h)], k[past, cols(h)], 1, 1)
                probs[odd][i, rows, past] = (score * wtab[odd][i, a - b]).astype(bf16)
        for a in range(nblk):
            rows = pl.ds(a * blk, blk)
            past = pl.ds(0, (a + 1) * blk)
            out[rows, cols(h)] = dot(probs[odd][i, rows, past], v[past, cols(h)], 1, 0)

    @pl.loop(0, pairs)
    def _(i):
        for odd in range(2):
            h = 2 * i + odd
            attend(h, odd, i)

            @pl.when(jnp.logical_and(first, (h >= 1) & (h <= pairs)))
            def _(h=h):
                accept_pair(forward, h - 1)

            if n_dp > 1:

                @pl.when(jnp.logical_and(first, h == shift))
                def _():
                    pl.semaphore_signal(turn, inc=1, device_id={"dp": 1 - md}, device_id_type=MESH)

    if n_dp > 1:

        @pl.when(jnp.logical_not(first))
        def _():
            pl.semaphore_wait(turn, 1)

            @pl.loop(0, pairs)
            def _(i):
                begin_pair(forward, i)

            begin_rest(forward)

    @pl.when(jnp.logical_not(first))
    def _():
        @pl.loop(0, pairs)
        def _(i):
            accept_pair(forward, i)

    middle(forward)
    for s in range(steps - 1):
        pl.semaphore_wait(ready.at[s], near_heads + (1 if square and s == 0 else 0))
        greet(ready.at[s + 1])

    loads[1].wait()
    for load in small[1:]:
        load.wait()

    token = mask_ref[...].astype(f32)
    at = me * slab + lax.broadcasted_iota(jnp.int32, (1, slab), 1)
    length = jnp.full((1, slab), len_ref[0], jnp.int32)
    token = token * (at < length).astype(f32) * jnp.minimum(imp_ref[...], clip_high)
    token = token * adv_ref[0] * (float(slab * n_seq) / length.astype(f32))

    squares[...] = jnp.zeros((slab, dim), f32)
    mixes[...] = jnp.zeros((slab, dim), f32)

    def widen(h):
        half = pref_f[h].astype(bf16)
        state[h] = half
        grow = up[h] * jnp.exp2(-rate(h, dim))
        full = out[:, cols(h)] + dot(q[:, cols(h)], half, 1, 0) * grow
        out[:, cols(h)] = full
        return full, c[:, cols(h)].astype(f32) * gain_ref[pl.ds(h, 1), :] * full

    @pl.loop(0, pairs - 1)
    def _(i):
        finish_even(forward, i)
        finish_odd(forward, i)
        full, mix = widen(2 * i)
        other, blend = widen(2 * i + 1)
        squares[...] += full * full + other * other
        mixes[...] += mix + blend

    finish_even(forward, pairs - 1)
    full, mix = widen(heads - 2)
    squares[...] += full * full
    mixes[...] += mix
    finish_odd(forward, pairs - 1)
    full, mix = widen(heads - 1)
    squares[...] += full * full
    mixes[...] += mix

    stat[mh, 0:1, :] = jnp.sum(squares[...].T, axis=0, keepdims=True)
    stat[mh, 1:2, :] = jnp.sum(mixes[...].T, axis=0, keepdims=True) * token
    posts = [
        pltpu.make_async_remote_copy(
            src_ref=stat.at[mh],
            dst_ref=stat.at[mh],
            send_sem=ss_sem.at[off - 1],
            recv_sem=sr_sem.at[off - 1],
            device_id={"head": lax.rem(mh + off, n_head)},
            device_id_type=MESH,
        )
        for off in range(1, n_head)
    ]
    pl.semaphore_wait(ready.at[steps - 1], near_heads + (1 if square and steps == 1 else 0))
    for post in posts:
        post.start()
    for post in posts:
        post.wait_recv()
    sums = stat[0]
    for i in range(1, n_head):
        sums = sums + stat[i]
    count = features * n_head
    inverse = lax.rsqrt(sums[0:1] / count + epsilon)
    mean = inverse * (sums[1:2] / count)

    def column(row):
        return jnp.broadcast_to(row, (dim, slab)).T

    inv_col = column(inverse)
    give_col = column(inverse * token)
    take_col = column(inverse * inverse * mean)

    def give(h):
        given = c[:, cols(h)].astype(f32) * give_col
        grad = (given * gain_ref[pl.ds(h, 1), :] - take_col * out[:, cols(h)]).astype(bf16)
        go[:, cols(h)] = grad
        faded = (q[:, cols(h)].astype(f32) * up[h]).astype(bf16)
        tot_b[0, h] = dot(faded, grad, 0, 0)

    give(0)
    begin_even(backward, 0)
    give(1)
    begin_odd(backward, 0)

    @pl.loop(1, pairs)
    def _(i):
        give(2 * i)
        give(2 * i + 1)
        begin_even(backward, i)
        begin_odd(backward, i)

    begin_rest(backward)

    @pl.loop(0, heads)
    def _(h):
        gain = gain_ref[pl.ds(h, 1), :]
        full = out[:, cols(h)]
        given = c[:, cols(h)].astype(f32) * give_col
        o_mix[0, :, cols(h)] = (full * inv_col * gain).astype(bf16)
        gsum[me, pl.ds(h, 1), :] = jnp.sum(given * full, axis=0, keepdims=True)

    shares = [
        pltpu.make_async_remote_copy(
            src_ref=gsum.at[me],
            dst_ref=gsum.at[me],
            send_sem=gs_sem.at[off],
            recv_sem=gr_sem.at[off],
            device_id={"seq": lax.rem(me + off, n_seq)},
            device_id_type=MESH,
        )
        for off in range(1, n_seq)
    ]
    swap = pltpu.make_async_remote_copy(
        src_ref=gpair.at[0],
        dst_ref=gpair.at[1],
        send_sem=gs_sem.at[0],
        recv_sem=gr_sem.at[0],
        device_id={"dp": lax.rem(md + 1, n_dp)},
        device_id_type=MESH,
    )
    for share in shares:
        share.start()
    late = min(1, pairs - 1)

    @pl.when(first)
    def _():
        accept_pair(backward, 0)

    @pl.loop(0, pairs)
    def _(i):
        for a in range(nblk):
            rows = pl.ds(a * blk, blk)
            for odd in range(2):
                h = 2 * i + odd
                grad = go[rows, cols(h)]
                for b in range(a + 1):
                    past = pl.ds(b * blk, blk)
                    score = dot(grad, v[past, cols(h)], 1, 1)
                    dsc[odd][rows, past] = (score * wtab[odd][i, a - b]).astype(bf16)
        for a in range(nblk):
            rows = pl.ds(a * blk, blk)
            past = pl.ds(0, (a + 1) * blk)
            for odd in range(2):
                h = 2 * i + odd
                grow = up[h, rows, :] * jnp.exp2(-rate(h, dim))
                total = dot(dsc[odd][rows, past], k[past, cols(h)], 1, 0)
                total = total + dot(go[rows, cols(h)], state[h], 1, 1) * grow
                o_dq[0, rows, cols(h)] = total.astype(bf16)
        for b in range(nblk):
            past = pl.ds(b * blk, blk)
            rest = pl.ds(b * blk, slab - b * blk)
            for odd in range(2):
                h = 2 * i + odd
                pk[past, cols(h)] = dot(dsc[odd][rest, past], q[rest, cols(h)], 0, 0)
                pv[past, cols(h)] = dot(probs[odd][i, rest, past], go[rest, cols(h)], 0, 0)

        for ahead in (1, 2):

            @pl.when(jnp.logical_and(first, 2 * i + ahead < pairs))
            def _(ahead=ahead):
                accept_pair(backward, 2 * i + ahead)

        @pl.when(jnp.logical_and(jnp.logical_not(first), i == late))
        def _():
            @pl.loop(0, late)
            def _(p):
                accept_pair(backward, p)

        @pl.when(jnp.logical_and(jnp.logical_not(first), i >= late))
        def _():
            accept_pair(backward, i)

    for share in shares:
        share.wait_recv()
    total = gsum[0]
    for s in range(1, n_seq):
        total = total + gsum[s]
    gpair[0] = total
    if n_dp > 1:
        swap.start()
    middle(backward)

    def close(h):
        half = pref_b[h].astype(bf16)
        fade = down[h] * jnp.exp2(-rate(h, dim))
        dk = pk[:, cols(h)] + dot(v[:, cols(h)], half, 1, 1) * fade
        o_dk[0, :, cols(h)] = dk.astype(bf16)
        dv = pv[:, cols(h)] + dot(k[:, cols(h)], half, 1, 0) * fade
        o_dv[0, :, cols(h)] = dv.astype(bf16)

    @pl.loop(0, pairs - 1)
    def _(i):
        finish_even(backward, i)
        finish_odd(backward, i)
        close(2 * i)
        close(2 * i + 1)

    finish_even(backward, pairs - 1)
    close(heads - 2)
    finish_odd(backward, pairs - 1)
    close(heads - 1)
    if n_dp > 1:
        swap.wait()
        gg_ref[...] = gpair[0] + gpair[1]
    else:
        gg_ref[...] = gpair[0]
    for post in posts + shares:
        post.wait_send()
    settle(forward)
    settle(backward)


def writer(n, *refs):
    sem = refs[-1]
    copies = [pltpu.make_async_copy(refs[i], refs[n + i], sem.at[i]) for i in range(n)]
    for copy in copies:
        copy.start()
    for copy in copies:
        copy.wait()


def on_device(
    n_seq,
    n_head,
    n_dp,
    query_rows,
    key_rows,
    value_rows,
    norm_gain,
    cotangent,
    loss_mask,
    importance,
    advantage,
    lengths,
    decay_index,
):
    batches, slab, features = query_rows.shape
    heads = decay_index.shape[0]
    dim = features // heads
    stages = n_seq.bit_length() - 1
    assert batches == 1 and heads % 2 == 0 and n_seq == 1 << stages and stages > 0 and n_dp <= 2
    vmem = pl.BlockSpec(memory_space=pltpu.VMEM)
    smem = pl.BlockSpec(memory_space=pltpu.SMEM)
    far = pl.BlockSpec(memory_space=pltpu.HBM)
    rows = jax.ShapeDtypeStruct(query_rows.shape, bf16)
    wide = pltpu.VMEM((slab, features), bf16)
    wide32 = pltpu.VMEM((slab, features), f32)
    blk = min(256, slab)
    states = pltpu.VMEM((stages, heads, dim, dim), f32)
    dma = pltpu.SemaphoreType.DMA

    def stay(array):
        return pltpu.with_memory_space_constraint(array, pltpu.HBM)

    results = pl.pallas_call(
        functools.partial(kernel, n_seq, n_head, n_dp),
        out_shape=(rows, rows, rows, rows, jax.ShapeDtypeStruct((heads, dim), f32)),
        in_specs=[far, smem, smem] + [far] * 7,
        out_specs=(vmem,) * 5,
        scratch_shapes=[
            pltpu.SMEM((heads,), jnp.int32),
            pltpu.VMEM((heads, dim), f32),
            pltpu.VMEM((1, slab), jnp.int32),
            pltpu.VMEM((1, slab), f32),
        ]
        + [wide] * 4
        + [wide32, wide, wide32, wide32]
        + [
            pltpu.VMEM((heads // 2, slab, slab), bf16),
            pltpu.VMEM((heads // 2, slab, slab), bf16),
            pltpu.VMEM((slab, slab), bf16),
            pltpu.VMEM((slab, slab), bf16),
            pltpu.VMEM((heads // 2, slab // blk, blk, blk), f32),
            pltpu.VMEM((heads // 2, slab // blk, blk, blk), f32),
            pltpu.VMEM((heads, slab, dim), f32),
            pltpu.VMEM((heads, slab, dim), f32),
            pltpu.VMEM((slab, dim), f32),
            pltpu.VMEM((slab, dim), f32),
            states,
            states,
            states,
            states,
            pltpu.VMEM((heads, dim, dim), f32),
            pltpu.VMEM((heads, dim, dim), f32),
            pltpu.VMEM((heads, dim, dim), bf16),
            pltpu.VMEM((n_head, 2, slab), f32),
            pltpu.VMEM((n_seq, heads, dim), f32),
            pltpu.VMEM((2, heads, dim), f32),
            dma((2,)),
            dma((2, heads // 2)),
            dma((4,)),
            dma((stages, heads)),
            dma((stages, heads)),
            dma((stages, heads)),
            dma((stages, heads)),
            dma((max(n_head - 1, 1),)),
            dma((max(n_head - 1, 1),)),
            dma((n_seq,)),
            dma((n_seq,)),
            pltpu.SemaphoreType.REGULAR,
            pltpu.SemaphoreType.REGULAR((max(n_head - 2, 1),)),
        ],
        compiler_params=pltpu.CompilerParams(
            collective_id=0, has_side_effects=True, vmem_limit_bytes=48 << 20
        ),
        name="lightning",
    )(
        stay(decay_index),
        advantage,
        lengths,
        stay(norm_gain.reshape(heads, dim)),
        stay(loss_mask),
        stay(importance),
        stay(query_rows),
        stay(key_rows),
        stay(value_rows),
        stay(cotangent),
    )
    shapes = tuple(jax.ShapeDtypeStruct(r.shape, r.dtype) for r in results)
    any_space = pl.BlockSpec(memory_space=pl.ANY)
    mixed, dq, dk, dv, gain_grad = pl.pallas_call(
        functools.partial(writer, len(shapes)),
        out_shape=shapes,
        in_specs=[vmem] * len(shapes),
        out_specs=(any_space,) * len(shapes),
        scratch_shapes=[dma((len(shapes),))],
        compiler_params=pltpu.CompilerParams(vmem_limit_bytes=8 << 20),
        name="writer",
    )(*results)
    return (mixed, dq, dk, dv, gain_grad.reshape(features))


def solution(mesh):
    wide = P("dp", "seq", "head")
    token = P("dp", "seq")
    in_specs = (wide, wide, wide, P("head"), wide, token, token, P("dp"), P("dp"), P("head"))
    out_specs = (wide, wide, wide, wide, P("head"))
    body = functools.partial(on_device, mesh.shape["seq"], mesh.shape["head"], mesh.shape["dp"])
    return jax.shard_map(
        body, mesh=mesh, in_specs=in_specs, out_specs=out_specs, check_vma=False
    )
```
